32 devices in a mesh: dp: 2 (over x), row: 4 (over z), col: 4 (over y, core).
Axes of the slice: x: 2, y: 2, z: 4, core: 2. Of those that a mesh axis runs over, the one named last changes fastest.
Arguments:
- tokens: bfloat16 [2, 1024, 1536], P(None, ('dp', 'col'), 'row'), may hold values from -12 to 12
- segments: int32 [2, 2, 512], P(None, 'dp'), may hold values from 0 to 11, never falling along the last dimension, each value on 1 to 256 neighbouring positions
- attn_gain: bfloat16 [1536], P('row'), may hold values from 0.25 to 1.75
- w_query: bfloat16 [1536, 1536], P('row', 'col'), may hold values from -0.3125 to 0.3125
- key_weight: bfloat16 [1536, 768], P('row', 'col'), may hold values from -0.15625 to 0.15625
- value_weight: bfloat16 [1536, 768], P('row', 'col'), may hold values from -0.15625 to 0.15625
- w_out: bfloat16 [1536, 1536], P('col', 'row'), may hold values from -0.4375 to 0.4375
- ffn_gain: bfloat16 [1536], P('row'), may hold values from 0.25 to 1.75
- w_gate: bfloat16 [1536, 4096], P('row', 'col'), may hold values from -0.15625 to 0.15625
- w_up: bfloat16 [1536, 4096], P('row', 'col'), may hold values from -0.15625 to 0.15625
- w_down: bfloat16 [4096, 1536], P('col', 'row'), may hold values from -0.125 to 0.125
- out_grad: bfloat16 [2, 1024, 1536], P(None, ('dp', 'col'), 'row'), may hold values from -6 to 6
Outputs:
- out_tokens: bfloat16 [2, 1024, 1536], P(None, ('dp', 'col'), 'row')
- in_grad: float32 [2, 1024, 1536], P(None, ('dp', 'col'), 'row')
- attn_gain_grad: float32 [1536], P('row')
- w_query_grad: float32 [1536, 1536], P('row', 'col')
- w_key_grad: float32 [1536, 768], P('row', 'col')
- w_value_grad: float32 [1536, 768], P('row', 'col')
- w_out_grad: float32 [1536, 1536], P('col', 'row')
- ffn_gain_grad: float32 [1536], P('row')
- w_gate_grad: float32 [1536, 4096], P('row', 'col')
- w_up_grad: float32 [1536, 4096], P('row', 'col')
- w_down_grad: float32 [4096, 1536], P('col', 'row')
The draws below stay inside these ranges and needn't reach their ends.
Inputs may be any that keep to these rules, and one draw needn't show every extreme that they name: `segments`: along each sequence the document numbers never fall; each of the 12 documents holds 1 to 256 tokens and one holds exactly 256.
All inputs are finite; a program needn't handle non-finite values.
Results may differ from the reference program's by a relative error of at most 0.019.
Values may be sent and summed in bfloat16 or wider, within the bound.
No kernel may reach another device: no remote copies, remote signals or barrier semaphores. Data moves between devices by JAX's collectives and lax.ppermute only.
A program may use at most 128 MiB of HBM per device.

```python
import math
import jax
import jax.numpy as jnp
import numpy as np
from jax import lax

MODEL_WIDTH = 1536
QUERY_HEADS = 16
KV_HEAD_COUNT = 8
HEAD_SIZE = 96
FF = 4096
MB = 2
DOCS = 12
LEN = 512
BATCH = 1024
N_DP = 2


def draw_tokens(key, part):
    base_key, column_key = jax.random.split(key, 2)
    column = jnp.arange(MODEL_WIDTH, dtype=jnp.float32) / MODEL_WIDTH
    spread = jax.random.uniform(column_key, (MODEL_WIDTH,), jnp.float32, 0.0, 1.0)
    column_scale = 0.3 * jnp.exp(math.log(3.0) * column + math.log(3.3) * spread)
    base = jnp.clip(jax.random.normal(base_key, (MB, BATCH, MODEL_WIDTH), jnp.float32), -4.0, 4.0)
    return (base * column_scale).astype(jnp.bfloat16)


def levels(own_key, shape, pieces, smallest, high):
    def one(axis_at, shards_of):
        steps = jax.random.uniform(jax.random.fold_in(jax.random.fold_in(own_key, 6), axis_at), (shards_of,), jnp.float32, smallest / len(pieces), high / len(pieces))
        return jnp.repeat(jnp.exp(steps), shape[axis_at] // shards_of).reshape((-1,) + (1,) * (len(shape) - axis_at - 1))

    loudness = one(*pieces[0])
    for cut in pieces[1:]:
        loudness = loudness * one(*cut)
    return loudness


def profile(amount, total, reach, slope):
    portions = [(1 << 20) // math.isqrt(standing ** slope) + 1 for standing in range(2, amount + 1)]
    spare, given = total - reach - (amount - 1), [1] * (amount - 1)
    while spare > 0:
        candidates = [i for i in range(amount - 1) if given[i] < reach]
        whole, budget = sum([portions[i] for i in candidates]), spare
        for i in candidates:
            addition = min(reach - given[i], max(1, budget * portions[i] // whole), spare)
            given[i] = given[i] + addition
            spare = spare - addition
    return np.array([reach] + given)


def ragged_sizes(stream_key, count, total, reach, skew):
    if count == 2:
        one = jax.random.randint(stream_key, (), max(1, total - reach), min(reach, total - 1) + 1)
        return jnp.stack([one, total - one])
    sizes = jnp.asarray(profile(count, total, reach, skew), jnp.int32)
    twos = (count - 1) // 2
    source_of, taker = sizes[1:1 + 2 * twos:2], sizes[2:2 + 2 * twos:2]
    room = jnp.minimum(source_of - 1, reach - taker)
    shifted = jax.random.randint(jax.random.fold_in(stream_key, 1), (twos,), 0, 1 << 20) % (room + 1)
    sizes = sizes.at[1:1 + 2 * twos:2].set(source_of - shifted).at[2:2 + 2 * twos:2].set(taker + shifted)
    return sizes[jax.random.permutation(jax.random.fold_in(stream_key, 2), count)]


def noise(own_key, dims, scale, bound, cuts=(), kind=jnp.bfloat16):
    values = jax.random.normal(own_key, dims, jnp.float32) * scale
    if len(cuts) > 0:
        values = levels(own_key, dims, cuts, -0.22, 0.18) * values
    return jnp.clip(values, min=-bound, max=bound).astype(kind)


def setup_inputs(seed: int = 0) -> dict:
    seeds = jax.random.split(jax.random.key(seed), 13)
    return {
        "tokens": draw_tokens(jax.random.fold_in(seeds[12], 71), 0),
        "segments": jax.vmap(lambda own: jnp.searchsorted(jnp.cumsum(ragged_sizes(own, DOCS, LEN, LEN // 2, 2)), jnp.arange(LEN), side="right"))(jax.random.split(seeds[1], MB * N_DP)).reshape((MB, N_DP, LEN)).astype(jnp.int32),
        "attn_gain": jnp.clip(1.0 + 0.15 * jax.random.normal(seeds[2], (MODEL_WIDTH,), jnp.float32), 0.25, 1.75).astype(jnp.bfloat16),
        "w_query": noise(seeds[3], (MODEL_WIDTH, QUERY_HEADS * HEAD_SIZE), (MODEL_WIDTH // 4) ** -0.5, 0.3125, ((0, 4), (1, 4))),
        "key_weight": noise(seeds[4], (MODEL_WIDTH, KV_HEAD_COUNT * HEAD_SIZE), MODEL_WIDTH ** -0.5, 0.15625, ((0, 4), (1, 4))),
        "value_weight": noise(seeds[5], (MODEL_WIDTH, KV_HEAD_COUNT * HEAD_SIZE), MODEL_WIDTH ** -0.5, 0.15625, ((0, 4), (1, 4))),
        "w_out": noise(seeds[6], (QUERY_HEADS * HEAD_SIZE, MODEL_WIDTH), (QUERY_HEADS * HEAD_SIZE // 8) ** -0.5, 0.4375, ((0, 4), (1, 4))),
        "ffn_gain": jnp.clip(1.0 + 0.15 * jax.random.normal(seeds[7], (MODEL_WIDTH,), jnp.float32), 0.25, 1.75).astype(jnp.bfloat16),
        "w_gate": noise(seeds[8], (MODEL_WIDTH, FF), MODEL_WIDTH ** -0.5, 0.15625, ((0, 4), (1, 4))),
        "w_up": noise(seeds[9], (MODEL_WIDTH, FF), MODEL_WIDTH ** -0.5, 0.15625, ((0, 4), (1, 4))),
        "w_down": noise(seeds[10], (FF, MODEL_WIDTH), (FF // 2) ** -0.5, 0.125, ((0, 4), (1, 4))),
        "out_grad": noise(seeds[11], (MB, BATCH, MODEL_WIDTH), 1.0, 6.0, ((1, 8), (2, 4))),
    }


EPSILON = 1e-05
ROPE_BASE = 100000.0
HIGHEST = lax.Precision.HIGHEST

@jax.custom_vjp
def reduced_precision(v):
    return lax.optimization_barrier(v.astype(jnp.bfloat16)).astype(jnp.float32)

@jax.custom_vjp
def reduced_backward(v):
    return v

def low_keep(v):
    return (reduced_precision(v), None)

def low_pass(kept, grad):
    return (grad,)

def back_keep(v):
    return (v, None)

def back_low(kept, grad):
    return (reduced_precision(grad),)
reduced_precision.defvjp(low_keep, low_pass)
reduced_backward.defvjp(back_keep, back_low)

def positions_of(seg_ids):
    token_length = seg_ids.shape[0]
    places = jnp.arange(token_length, dtype=jnp.int32)
    previous = jnp.concatenate([seg_ids[:1] - 1, seg_ids[:-1]])
    starts = jnp.where(seg_ids != previous, places, 0)
    return places - lax.cummax(starts, axis=0)

def rope_tables(position):
    half_width = HEAD_SIZE // 2
    frequency = ROPE_BASE ** (-(jnp.arange(half_width, dtype=jnp.float32) * 2.0 / HEAD_SIZE))
    angles = position.astype(jnp.float32)[:, None] * frequency[None, :]
    return (jnp.cos(angles)[:, None, :], jnp.sin(angles)[:, None, :])

def rotate(values, cosine, sine_table, direction):
    half_width = values.shape[-1] // 2
    first_half = values[..., :half_width]
    second_half = values[..., half_width:]
    return jnp.concatenate([first_half * cosine - direction * second_half * sine_table, second_half * cosine + direction * first_half * sine_table], axis=-1)

def matrix_product(left_op, right_op):
    return jnp.dot(left_op, right_op, precision=HIGHEST)

def normed(residual, gain_vec):
    inverse = lax.rsqrt(lax.optimization_barrier(jnp.mean(residual * residual, axis=-1, keepdims=True)) + EPSILON)
    return reduced_precision(residual * inverse * gain_vec)

def forward(residual, weights, seg_ids):
    attn_gain, w_query, key_weight, value_weight, w_out, ffn_gain, w_gate, w_up, w_down = weights
    token_length = residual.shape[0]
    cosine, sine_table = rope_tables(positions_of(seg_ids))
    first_normed_input = normed(residual, attn_gain)
    query_rows = reduced_backward(matrix_product(first_normed_input, w_query)).reshape(token_length, QUERY_HEADS, HEAD_SIZE)
    linear_key_rows = reduced_backward(matrix_product(first_normed_input, key_weight)).reshape(token_length, KV_HEAD_COUNT, HEAD_SIZE)
    value_rows_full = reduced_precision(reduced_backward(matrix_product(first_normed_input, value_weight))).reshape(token_length, KV_HEAD_COUNT, HEAD_SIZE)
    scaled_input = reduced_precision(rotate(query_rows, cosine, sine_table, 1.0) * HEAD_SIZE ** (-0.5))
    keys_rot = reduced_precision(rotate(linear_key_rows, cosine, sine_table, 1.0))
    places = jnp.arange(token_length, dtype=jnp.int32)
    allowed = (seg_ids[:, None] == seg_ids[None, :]) & (places[None, :] <= places[:, None])
    query_group_width = QUERY_HEADS // KV_HEAD_COUNT
    query_head_rows = scaled_input.reshape(token_length, KV_HEAD_COUNT, query_group_width, HEAD_SIZE).transpose(1, 2, 0, 3)
    key_heads = keys_rot.transpose(1, 0, 2)
    value_heads = value_rows_full.transpose(1, 0, 2)

    def one_group(operands):
        query_part, key_part, value_part = operands
        scores = reduced_backward(jnp.einsum('gqd,kd->gqk', query_part, key_part, precision=HIGHEST))
        scores = jnp.where(allowed[None], scores, -1e+30)
        exponent = jnp.exp(scores - lax.optimization_barrier(jnp.max(scores, axis=-1, keepdims=True)))
        probs = exponent / lax.optimization_barrier(jnp.sum(exponent, axis=-1, keepdims=True))
        return jnp.einsum('gqk,kd->gqd', reduced_precision(probs), value_part, precision=HIGHEST)
    head_out = lax.map(jax.checkpoint(one_group), (query_head_rows, key_heads, value_heads))
    attended = reduced_precision(reduced_backward(head_out.transpose(2, 0, 1, 3).reshape(token_length, QUERY_HEADS * HEAD_SIZE)))
    resid_mid = residual + reduced_backward(matrix_product(attended, w_out))
    normed_two = normed(resid_mid, ffn_gain)
    gate_lin = reduced_backward(matrix_product(normed_two, w_gate))
    up_lin = reduced_backward(matrix_product(normed_two, w_up))
    hidden = reduced_precision(gate_lin * jax.nn.sigmoid(gate_lin) * up_lin)
    return resid_mid + matrix_product(hidden, w_down)

def reference(tokens, segments, attn_gain, w_query, key_weight, value_weight, w_out, ffn_gain, w_gate, w_up, w_down, out_grad):
    seq_count = MB * N_DP
    inputs = tokens.astype(jnp.float32).reshape(seq_count, LEN, MODEL_WIDTH)
    cotangents = out_grad.astype(jnp.float32).reshape(seq_count, LEN, MODEL_WIDTH)
    seg_rows = segments.reshape(seq_count, LEN)
    params = (attn_gain.astype(jnp.float32), w_query.astype(jnp.float32), key_weight.astype(jnp.float32), value_weight.astype(jnp.float32), w_out.astype(jnp.float32), ffn_gain.astype(jnp.float32), w_gate.astype(jnp.float32), w_up.astype(jnp.float32), w_down.astype(jnp.float32))

    def one_sequence(totals, sequence):
        resid_in, cotangent, seg_ids = sequence

        def apply_layer(resid_arg, weight_arg):
            return forward(resid_arg, weight_arg, seg_ids)
        outputs, pullback = jax.vjp(apply_layer, resid_in, params)
        grad_resid, grad_params = pullback(cotangent)
        totals = tuple((total_part + grad_part for total_part, grad_part in zip(totals, grad_params)))
        return (totals, (outputs.astype(jnp.bfloat16), grad_resid))
    zero_grads = tuple((jnp.zeros(param.shape, jnp.float32) for param in params))
    totals, (outputs, in_grads) = lax.scan(one_sequence, zero_grads, (inputs, cotangents, seg_rows))
    return (outputs.reshape(MB, BATCH, MODEL_WIDTH), in_grads.reshape(MB, BATCH, MODEL_WIDTH), totals[0], totals[1], totals[2], totals[3], totals[4], totals[5], totals[6], totals[7], totals[8])
```

```python
import functools

import jax
import jax.numpy as jnp
from jax import lax
from jax.experimental import pallas as pl
from jax.experimental.pallas import tpu as pltpu
from jax.sharding import PartitionSpec as P

MODEL_WIDTH = 1536
QUERY_HEADS = 16
KV_HEAD_COUNT = 8
HEAD_SIZE = 96


EPSILON = 1e-05
ROPE_BASE = 100000.0


def positions_of(seg_ids):
    token_length = seg_ids.shape[0]
    places = jnp.arange(token_length, dtype=jnp.int32)
    previous = jnp.concatenate([seg_ids[:1] - 1, seg_ids[:-1]])
    starts = jnp.where(seg_ids != previous, places, 0)
    return places - lax.cummax(starts, axis=0)


def rope_tables(position):
    half_width = HEAD_SIZE // 2
    frequency = ROPE_BASE ** (-(jnp.arange(half_width, dtype=jnp.float32) * 2.0 / HEAD_SIZE))
    angles = position.astype(jnp.float32)[:, None] * frequency[None, :]
    return (jnp.cos(angles)[:, None, :], jnp.sin(angles)[:, None, :])


def rotate(values, cosine, sine_table, direction):
    half_width = values.shape[-1] // 2
    first_half = values[..., :half_width]
    second_half = values[..., half_width:]
    return jnp.concatenate(
        [
            first_half * cosine - direction * second_half * sine_table,
            second_half * cosine + direction * first_half * sine_table,
        ],
        axis=-1,
    )


def gather_cols(block):
    return lax.all_gather(block, "col", axis=0, tiled=True)


def gather_rows(block):
    return lax.all_gather(block, "row", axis=0, tiled=True)


def sum_rows(gathered, matrix):

    def partial_term(first_row, count_of_rows):
        return jnp.dot(gathered, matrix, preferred_element_type=jnp.float32)

    return lax.psum_scatter(
        partial_term(
            jnp.int32(0), lax.axis_size("row") * (gathered.shape[0] // lax.axis_size("row"))
        ),
        "row",
        scatter_dimension=0,
        tiled=True,
    )


def sum_cols(gathered, matrix):

    def partial_term(first_row, count_of_rows):
        return jnp.dot(gathered, matrix, preferred_element_type=jnp.float32)

    return lax.psum_scatter(
        partial_term(
            jnp.int32(0), lax.axis_size("col") * (gathered.shape[0] // lax.axis_size("col"))
        ),
        "col",
        scatter_dimension=0,
        tiled=True,
    )


def row_total(values):
    return lax.psum(values, "row")


def gather_keys(key_own, value_own):
    return (
        lax.all_gather(key_own, "row", axis=0, tiled=True),
        lax.all_gather(value_own, "row", axis=0, tiled=True),
    )


def scatter_keys(grad_keys, grad_values):
    return (
        lax.psum_scatter(
            grad_keys.astype(jnp.bfloat16), "row", scatter_dimension=0, tiled=True
        ).astype(jnp.float32),
        lax.psum_scatter(
            grad_values.astype(jnp.bfloat16), "row", scatter_dimension=0, tiled=True
        ).astype(jnp.float32),
    )


def weight_grad(left_op, right_op):
    return lax.dot_general(
        left_op, right_op, (((0,), (0,)), ((), ())), preferred_element_type=jnp.float32
    )


def reduce_weights(parts):
    return (
        lax.psum(parts[0].astype(jnp.bfloat16), "dp").astype(jnp.float32),
        lax.psum(parts[1].astype(jnp.bfloat16), "dp").astype(jnp.float32),
        lax.psum(parts[2].astype(jnp.bfloat16), "dp").astype(jnp.float32),
        lax.psum(parts[3].astype(jnp.bfloat16), "dp").astype(jnp.float32),
    )


def reduce_gains(parts):
    return lax.psum((parts[0], parts[1]), ("dp", "col"))


def finish(weight_parts, gain_parts):
    return (reduce_weights(weight_parts), reduce_gains(gain_parts))


def masked_scores(grouped_query, key_heads, allowed):
    scores = jnp.einsum(
        "qcgd,kcd->cgqk", grouped_query, key_heads, preferred_element_type=jnp.float32
    )
    return jnp.where(allowed[None, None], scores, -1e30)


def project_heads(projected, cos_rows, sin_rows, width_query, width_kv):
    count_of_rows = projected.shape[0]
    local_key_value = width_kv // HEAD_SIZE
    query_lin = projected[:, :width_query].reshape(
        count_of_rows, width_query // HEAD_SIZE, HEAD_SIZE
    )
    key_lin = projected[:, width_query : width_query + width_kv].reshape(
        count_of_rows, local_key_value, HEAD_SIZE
    )
    query_rows = (rotate(query_lin, cos_rows, sin_rows, 1.0) * HEAD_SIZE ** (-0.5)).astype(
        jnp.bfloat16
    )
    grouped_query = query_rows.reshape(
        count_of_rows, local_key_value, QUERY_HEADS // KV_HEAD_COUNT, HEAD_SIZE
    )
    key_own = (
        rotate(key_lin, cos_rows, sin_rows, 1.0)
        .astype(jnp.bfloat16)
        .reshape(count_of_rows, width_kv)
    )
    value_own = projected[:, width_query + width_kv :].astype(jnp.bfloat16)
    return (grouped_query, key_own, value_own)


def attend(grouped_query, key_heads, value_heads, allowed):
    scores = masked_scores(grouped_query, key_heads, allowed)
    top_score = jnp.max(scores, axis=-1, keepdims=True)
    exponent = jnp.exp(scores - top_score)
    sum_exp = jnp.sum(exponent, axis=-1, keepdims=True)
    attn_probs = exponent / sum_exp
    attended = jnp.einsum(
        "cgqk,kcd->qcgd",
        attn_probs.astype(jnp.bfloat16),
        value_heads,
        preferred_element_type=jnp.float32,
    )
    count_of_rows = grouped_query.shape[0]
    return (attended.reshape(count_of_rows, -1).astype(jnp.bfloat16), top_score + jnp.log(sum_exp))


def attend_back(grad_attn, grouped_query, key_heads, value_heads, allowed, log_total):
    seq_len = key_heads.shape[0]
    grad_attended = grad_attn.astype(jnp.bfloat16).reshape(grouped_query.shape)
    probs_again = jnp.exp(masked_scores(grouped_query, key_heads, allowed) - log_total)
    grad_probs = jnp.einsum(
        "qcgd,kcd->cgqk", grad_attended, value_heads, preferred_element_type=jnp.float32
    )
    row_delta = jnp.sum(probs_again * grad_probs, axis=-1, keepdims=True)
    grad_scores = (probs_again * (grad_probs - row_delta)).astype(jnp.bfloat16)
    grad_value_all = jnp.einsum(
        "cgqk,qcgd->kcd",
        probs_again.astype(jnp.bfloat16),
        grad_attended,
        preferred_element_type=jnp.float32,
    )
    grad_query = jnp.einsum(
        "cgqk,kcd->qcgd", grad_scores, key_heads, preferred_element_type=jnp.float32
    )
    grad_key_all = jnp.einsum(
        "cgqk,qcgd->kcd", grad_scores, grouped_query, preferred_element_type=jnp.float32
    )
    return (grad_query, grad_key_all.reshape(seq_len, -1), grad_value_all.reshape(seq_len, -1))


def head_grads(grad_query, grad_key_own, grad_value_own, cos_rows, sin_rows):
    count_of_rows = grad_query.shape[0]
    grad_query_lin = rotate(
        grad_query.reshape(count_of_rows, -1, HEAD_SIZE) * HEAD_SIZE ** (-0.5),
        cos_rows,
        sin_rows,
        -1.0,
    )
    grad_key_lin = rotate(
        grad_key_own.reshape(count_of_rows, -1, HEAD_SIZE), cos_rows, sin_rows, -1.0
    )
    return jnp.concatenate(
        [
            grad_query_lin.reshape(count_of_rows, -1),
            grad_key_lin.reshape(count_of_rows, -1),
            grad_value_own,
        ],
        axis=1,
    ).astype(jnp.bfloat16)


def blocked_step(resid_in, grad_top, seg_all, cos_all, sin_all, weight_set, norm_gains, widths):
    w_qkv, w_out, w_pair, w_down = weight_set
    gain_one, gain_two = norm_gains
    width_query, width_kv, width_ff = widths
    seq_len = resid_in.shape[0] * lax.axis_size("col")
    own_rows = seq_len // lax.axis_size("row")
    own_start = lax.axis_index("row") * own_rows
    cos_own = lax.dynamic_slice_in_dim(cos_all, own_start, own_rows, 0)
    sin_own = lax.dynamic_slice_in_dim(sin_all, own_start, own_rows, 0)
    seg_own = lax.dynamic_slice_in_dim(seg_all, own_start, own_rows, 0)
    query_pos = own_start + jnp.arange(own_rows, dtype=jnp.int32)
    key_pos = jnp.arange(seq_len, dtype=jnp.int32)
    allowed = (seg_own[:, None] == seg_all[None, :]) & (key_pos[None, :] <= query_pos[:, None])
    inverse_one = lax.rsqrt(row_total(jnp.sum(resid_in * resid_in, axis=1)) / MODEL_WIDTH + EPSILON)
    first_normed_input = (resid_in * inverse_one[:, None] * gain_one).astype(jnp.bfloat16)
    gathered_one = gather_cols(first_normed_input)
    projected = sum_rows(gathered_one, w_qkv)
    grouped_query, key_own, value_own = project_heads(
        projected, cos_own, sin_own, width_query, width_kv
    )
    key_all, value_all = gather_keys(key_own, value_own)
    key_heads = key_all.reshape(seq_len, -1, HEAD_SIZE)
    value_heads = value_all.reshape(seq_len, -1, HEAD_SIZE)
    attn_rows, log_total = attend(grouped_query, key_heads, value_heads, allowed)
    gathered_attn = gather_rows(attn_rows)
    resid_mid = resid_in + sum_cols(gathered_attn, w_out)
    inverse_two = lax.rsqrt(
        row_total(jnp.sum(resid_mid * resid_mid, axis=1)) / MODEL_WIDTH + EPSILON
    )
    normed_two = (resid_mid * inverse_two[:, None] * gain_two).astype(jnp.bfloat16)
    gathered_two = gather_cols(normed_two)
    pair_lin = sum_rows(gathered_two, w_pair)
    gate_lin = pair_lin[:, :width_ff]
    up_lin = pair_lin[:, width_ff:]
    gate_sig = jax.nn.sigmoid(gate_lin)
    hidden = (gate_lin * gate_sig * up_lin).astype(jnp.bfloat16)
    gathered_hidden = gather_rows(hidden)
    block_out = resid_mid + sum_cols(gathered_hidden, w_down)
    gathered_grad = gather_cols(grad_top)
    grad_hidden = sum_rows(gathered_grad, w_down.T)
    local_down = weight_grad(gathered_hidden, gathered_grad)
    slope_term = gate_sig * (1.0 + gate_lin * (1.0 - gate_sig))
    grad_pair_rows = jnp.concatenate(
        [grad_hidden * up_lin * slope_term, grad_hidden * gate_lin * gate_sig], axis=1
    ).astype(jnp.bfloat16)
    gathered_pair = gather_rows(grad_pair_rows)
    grad_normed_two = sum_cols(gathered_pair, w_pair.T)
    local_pair = weight_grad(gathered_two, gathered_pair)
    scaled_two = grad_normed_two * gain_two
    stat_two = row_total(jnp.sum(scaled_two * resid_mid, axis=1))
    grad_mid = (
        grad_top.astype(jnp.float32)
        + inverse_two[:, None] * scaled_two
        - resid_mid * (inverse_two**3 * stat_two / MODEL_WIDTH)[:, None]
    )
    local_gain_two = jnp.sum(grad_normed_two * resid_mid * inverse_two[:, None], axis=0)
    gathered_mid = gather_cols(grad_mid.astype(jnp.bfloat16))
    grad_attn = sum_rows(gathered_mid, w_out.T)
    local_out = weight_grad(gathered_attn, gathered_mid)
    grad_query, grad_key_all, grad_value_all = attend_back(
        grad_attn, grouped_query, key_heads, value_heads, allowed, log_total
    )
    grad_key_own, grad_value_own = scatter_keys(grad_key_all, grad_value_all)
    grad_qkv_rows = head_grads(grad_query, grad_key_own, grad_value_own, cos_own, sin_own)
    gathered_qkv = gather_rows(grad_qkv_rows)
    grad_normed_one = sum_cols(gathered_qkv, w_qkv.T)
    local_qkv = weight_grad(gathered_one, gathered_qkv)
    scaled_one = grad_normed_one * gain_one
    stat_one = row_total(jnp.sum(scaled_one * resid_in, axis=1))
    grad_input = (
        grad_mid
        + inverse_one[:, None] * scaled_one
        - resid_in * (inverse_one**3 * stat_one / MODEL_WIDTH)[:, None]
    )
    local_gain_one = jnp.sum(grad_normed_one * resid_in * inverse_one[:, None], axis=0)
    return (
        block_out.astype(jnp.bfloat16),
        grad_input,
        (local_qkv, local_out, local_pair, local_down),
        (local_gain_one, local_gain_two),
    )


def local(
    tokens,
    segments,
    attn_gain,
    w_query,
    key_weight,
    value_weight,
    w_out,
    ffn_gain,
    w_gate,
    w_up,
    w_down,
    out_grad,
):
    micro_count = tokens.shape[0]
    width_query = w_query.shape[1]
    width_kv = key_weight.shape[1]
    width_ff = w_gate.shape[1]
    widths = (width_query, width_kv, width_ff)
    w_qkv = jnp.concatenate([w_query, key_weight, value_weight], axis=1)
    w_pair = jnp.concatenate([w_gate, w_up], axis=1)
    step_tokens, step_grads = (tokens, out_grad)
    weight_set = (w_qkv, w_out, w_pair, w_down)
    norm_gains = (attn_gain.astype(jnp.float32), ffn_gain.astype(jnp.float32))
    weight_totals = None
    gain_totals = None
    outputs = []
    in_grads = []
    for micro_step in range(micro_count):
        seg_all = segments[micro_step, 0]
        cos_all, sin_all = rope_tables(positions_of(seg_all))
        resid_in = step_tokens[micro_step].astype(jnp.float32)
        grad_top = step_grads[micro_step]
        results = blocked_step(
            resid_in, grad_top, seg_all, cos_all, sin_all, weight_set, norm_gains, widths
        )
        block_out, grad_input, local_weights, local_gains = results
        outputs.append(block_out)
        in_grads.append(grad_input)
        if weight_totals is None:
            weight_totals = tuple(local_weights)
            gain_totals = tuple(local_gains)
        else:
            weight_totals = tuple(
                (
                    total_part + local_part
                    for total_part, local_part in zip(weight_totals, local_weights)
                )
            )
            gain_totals = tuple(
                (
                    total_part + local_part
                    for total_part, local_part in zip(gain_totals, local_gains)
                )
            )
    weight_totals, gain_totals = finish(weight_totals, gain_totals)
    out_stack = jnp.stack(outputs)
    grad_stack = jnp.stack(in_grads)
    grad_qkv_total = weight_totals[0]
    grad_pair_total = weight_totals[2]
    return (
        out_stack,
        grad_stack,
        gain_totals[0],
        grad_qkv_total[:, :width_query],
        grad_qkv_total[:, width_query : width_query + width_kv],
        grad_qkv_total[:, width_query + width_kv :],
        weight_totals[1],
        gain_totals[1],
        grad_pair_total[:, :width_ff],
        grad_pair_total[:, width_ff:],
        weight_totals[3],
    )

EXCHANGE_ROWS = 16


def shift_rows(block, step):
    size = lax.axis_size("row")
    return lax.ppermute(block, "row", [(i, (i + step) % size) for i in range(size)])


def swap_cols(block, mask):
    return lax.ppermute(block, "col", [(i, i ^ mask) for i in range(lax.axis_size("col"))])


def swap_dp(block):
    return lax.ppermute(block, "dp", [(0, 1), (1, 0)])


def gather_fine(block):
    own = [block] + [shift_rows(block, step) for step in (1, 2, 3)]
    across = [swap_cols(piece, 2) for piece in own]
    pair = [swap_cols(piece, 1) for piece in own]
    far = [swap_cols(piece, 1) for piece in across]
    return own + pair + across + far


def gather_coarse(block):
    own = jnp.stack([block] + [shift_rows(block, step) for step in (1, 2, 3)])
    across = swap_cols(own, 2)
    return [own, swap_cols(own, 1), across, swap_cols(across, 1)]


def wide(value):
    return value.astype(jnp.float32)


def narrow(value):
    return value.astype(jnp.bfloat16)


def scatter_fine(parts):
    own_part, pair_part, across_part, far_part = parts
    from_far = swap_cols(far_part, 1)
    from_pair = swap_cols(pair_part, 1)
    total = None
    for step in (2, 1, 3, 0):
        sent = swap_cols(narrow(wide(across_part[step]) + wide(from_far[step])), 2)
        piece = wide(own_part[step]) + wide(from_pair[step]) + wide(sent)
        if step:
            piece = wide(shift_rows(narrow(piece), step))
        total = piece if total is None else total + piece
    return total


def scatter_coarse(parts):
    own_part, pair_part, across_part, far_part = parts
    from_far = swap_cols(far_part, 1)
    from_pair = swap_cols(pair_part, 1)
    sent = swap_cols(narrow(wide(across_part) + wide(from_far)), 2)
    piece = wide(own_part) + wide(from_pair) + wide(sent)
    total = piece[0]
    for step in (1, 2, 3):
        total = total + wide(shift_rows(narrow(piece[step]), step))
    return total


def mm(left, right):
    return lax.dot_general(
        left, right, (((1,), (0,)), ((), ())), preferred_element_type=jnp.float32
    )


def mm_nt(left, right):
    return lax.dot_general(
        left, right, (((1,), (1,)), ((), ())), preferred_element_type=jnp.float32
    )


def mm_tn(left, right):
    return lax.dot_general(
        left, right, (((0,), (0,)), ((), ())), preferred_element_type=jnp.float32
    )


def call(body, outs, *operands, flops=1 << 30):
    moved = sum(o.size * o.dtype.itemsize for o in operands)
    moved += sum(o.size * o.dtype.itemsize for o in outs)
    specs = [
        pl.BlockSpec(memory_space=pltpu.SMEM if o.ndim == 1 else pltpu.VMEM) for o in operands
    ]
    return pl.pallas_call(
        body,
        out_shape=outs,
        in_specs=specs,
        out_specs=[pl.BlockSpec(memory_space=pltpu.VMEM) for _ in outs],
        cost_estimate=pl.CostEstimate(flops=flops, bytes_accessed=moved, transcendentals=0),
    )(*operands)


def shaped(shape, dtype=jnp.bfloat16):
    return jax.ShapeDtypeStruct(shape, dtype)


def piece_of(group, block, step):
    if len(group) == 4:
        return group[block][step]
    return group[4 * block + step][...]


def normed_blocks(group, gain_ref, normed_ref, own_ref, rows, width):
    for block in range(4):
        pieces = [wide(piece_of(group, block, step)) for step in range(4)]
        square = sum(jnp.sum(p * p, axis=1, keepdims=True) for p in pieces)
        inverse = lax.rsqrt(square / MODEL_WIDTH + EPSILON)
        if block == 0:
            own_ref[...] = inverse
        for step in range(4):
            normed_ref[block * rows : (block + 1) * rows, step * width : (step + 1) * width] = (
                narrow(pieces[step] * inverse * gain_ref[step : step + 1, :])
            )


def store_parts(refs, product, step, rows):
    for block in range(4):
        refs[block][(4 - step) % 4, :rows, :] = narrow(product[block * rows : (block + 1) * rows])


def store_sums(refs, products, rows):
    ones = jnp.ones((8, products.shape[1]), jnp.bfloat16)
    high = narrow(products)
    low = narrow(products - wide(high))
    sums = mm_nt(ones, high) + mm_nt(ones, low)
    for block in range(4):
        for step in range(4):
            refs[block][step, rows:, :] = jnp.zeros(
                (EXCHANGE_ROWS, refs[block].shape[2]), jnp.bfloat16
            )
            refs[block][step, rows : rows + 1, :rows] = narrow(
                sums[0:1, block * rows : (block + 1) * rows]
            )


def head_kernel(place_ref, wq_ref, wk_ref, wv_ref, own_ref, one_ref, two_ref, three_ref):
    row = place_ref[0]
    half = place_ref[1]
    half_width = HEAD_SIZE // 2

    def pick(count, head, turned):
        source = lax.broadcasted_iota(jnp.int32, (count, 128), 0)
        lane = lax.broadcasted_iota(jnp.int32, (count, 128), 1)
        if turned:
            feature = jnp.where(lane < 64, lane, lane - 64 + half_width)
            used = (lane < half_width) | ((lane >= 64) & (lane < 64 + half_width))
        else:
            feature, used = (lane, lane < HEAD_SIZE)
        return narrow(jnp.where((source == head * HEAD_SIZE + feature) & used, 1.0, 0.0))

    for step, out_ref in enumerate((own_ref, one_ref, two_ref, three_ref)):
        head = lax.rem(row + step, 4)
        rows = out_ref.shape[0]
        window = (
            pl.ds(pl.multiple_of(half * rows, rows), rows) if step else pl.ds(0, rows)
        )
        out_ref[:, 0:128] = narrow(mm(wq_ref[window, :], pick(wq_ref.shape[1], head, True)))
        pair = lax.div(head, 2)
        out_ref[:, 128:256] = narrow(mm(wk_ref[window, :], pick(wk_ref.shape[1], pair, True)))
        out_ref[:, 256:384] = narrow(mm(wv_ref[window, :], pick(wv_ref.shape[1], pair, False)))


def attend_kernel(rows, width, *refs):
    group, refs = (refs[:16], refs[16:])
    gain_ref, refs = (refs[0], refs[1:])
    w_in, w_out, refs = (refs[:4], refs[4:8], refs[8:])
    cos_ref, sin_ref, start_ref, place_ref, key_ref = refs[:5]
    parts = refs[5:9]
    normed_ref, heads_ref, probs_ref, attn_ref, inverse_ref = refs[9:]
    normed_blocks(group, gain_ref, normed_ref, inverse_ref, rows, width)
    lin = sum(mm(normed_ref[:, s * width : (s + 1) * width], w_in[s][...]) for s in range(4))
    cos_t = cos_ref[...]
    sin_t = sin_ref[...]
    query, key = (lin[:, :128], lin[:, 128:256])
    query = query * cos_t + pltpu.roll(query, 64, 1) * sin_t
    key = narrow(key * cos_t + pltpu.roll(key, 64, 1) * sin_t)
    heads_ref[:, 0:128] = narrow(query * HEAD_SIZE ** (-0.5))
    heads_ref[:, 128:256] = key
    value = narrow(lin[:, 256:384])
    heads_ref[:, 256:384] = value
    for block in range(4):
        sl = slice(block * rows, (block + 1) * rows)
        scores = mm_nt(heads_ref[sl, 0:128], key)
        allowed = (key_ref[...] >= start_ref[sl, :]) & (key_ref[...] <= place_ref[sl, :])
        scores = jnp.where(allowed, scores, -1e30)
        exponent = jnp.exp(scores - jnp.max(scores, axis=1, keepdims=True))
        probs = narrow(exponent / jnp.sum(exponent, axis=1, keepdims=True))
        probs_ref[sl, :] = probs
        attn_ref[sl, :] = narrow(mm(probs, value))
    attn = attn_ref[:, :HEAD_SIZE]
    for step in range(4):
        store_parts(parts, mm(attn, w_out[step][...]), step, rows)


def feed_kernel(rows, width, *refs):
    group, grads, refs = (refs[:16], refs[16:20], refs[20:])
    gain_ref, refs = (refs[0], refs[1:])
    pair_w = (refs[0:4], refs[4:8])
    down_w = (refs[8:12], refs[12:16])
    refs = refs[16:]
    out_parts, grad_parts = (refs[:4], refs[4:8])
    normed_ref, hidden_ref, grad_pair_ref, inverse_ref, stat_ref = refs[8:]
    normed_blocks(group, gain_ref, normed_ref, inverse_ref, rows, width)
    units = down_w[0][0].shape[0]
    for half in range(2):
        lin = sum(
            mm(normed_ref[:, s * width : (s + 1) * width], pair_w[half][s][...]) for s in range(4)
        )
        gate, up = (lin[:, :units], lin[:, units:])
        grad_hidden = jnp.concatenate(
            [
                sum(mm_nt(grads[b][s], down_w[half][s][...]) for s in range(4))
                for b in range(4)
            ],
            axis=0,
        )
        sig = jax.nn.sigmoid(gate)
        hidden_ref[:, half * units : (half + 1) * units] = narrow(gate * sig * up)
        grad_gate = narrow(grad_hidden * up * (sig * (1.0 + gate * (1.0 - sig))))
        grad_up = narrow(grad_hidden * gate * sig)
        grad_pair_ref[:, 2 * half * units : (2 * half + 1) * units] = grad_gate
        grad_pair_ref[:, (2 * half + 1) * units : (2 * half + 2) * units] = grad_up
        term = wide(grad_gate) * gate + wide(grad_up) * up
        if half:
            stat_ref[...] += term
        else:
            stat_ref[...] = term
    for step in range(4):
        product = sum(
            mm_nt(
                grad_pair_ref[:, 2 * half * units : 2 * (half + 1) * units],
                pair_w[half][step][...],
            )
            for half in range(2)
        )
        store_parts(grad_parts, product, step, rows)
    store_sums(grad_parts, stat_ref[...], rows)
    for step in range(4):
        product = sum(
            mm(hidden_ref[:, half * units : (half + 1) * units], down_w[half][step][...])
            for half in range(2)
        )
        store_parts(out_parts, product, step, rows)


def attend_back_kernel(rows, width, *refs):
    group, refs = (refs[:16], refs[16:])
    w_in, w_out, refs = (refs[:4], refs[4:8], refs[8:])
    cos_ref, sin_ref, heads_ref, probs_ref = refs[:4]
    parts = refs[4:8]
    grad_heads_ref, grad_attn_ref, grad_scores_ref = refs[8:]
    for block in range(4):
        grad_attn_ref[block * rows : (block + 1) * rows, :] = narrow(
            sum(mm_nt(piece_of(group, block, s), w_out[s][...]) for s in range(4))
        )
    grad_attn = grad_attn_ref[...]
    value = heads_ref[:, 256 : 256 + HEAD_SIZE]
    for block in range(4):
        sl = slice(block * rows, (block + 1) * rows)
        probs = wide(probs_ref[sl, :])
        weighted = mm_nt(grad_attn_ref[sl, :], value)
        delta = jnp.sum(probs * weighted, axis=1, keepdims=True)
        grad_scores_ref[sl, :] = narrow(probs * (weighted - delta))
    grad_scores = grad_scores_ref[...]
    query, key = (heads_ref[:, 0:128], heads_ref[:, 128:256])
    grad_query = mm(grad_scores, key)
    grad_key = mm_tn(grad_scores, query)
    grad_value = mm_tn(probs_ref[...], grad_attn)
    stat = grad_query * wide(query) + grad_key * wide(key)
    pad = jnp.zeros((grad_value.shape[0], 128 - HEAD_SIZE), jnp.float32)
    grad_value = jnp.concatenate([grad_value, pad], axis=1)
    stat = stat + grad_value * wide(heads_ref[:, 256:384])
    cos_t = cos_ref[...]
    sin_t = sin_ref[...]
    scale = HEAD_SIZE ** (-0.5)
    grad_heads_ref[:, 0:128] = narrow(
        (grad_query * cos_t - pltpu.roll(grad_query, 64, 1) * sin_t) * scale
    )
    grad_heads_ref[:, 128:256] = narrow(grad_key * cos_t - pltpu.roll(grad_key, 64, 1) * sin_t)
    grad_heads_ref[:, 256:384] = narrow(grad_value)
    grad_heads = grad_heads_ref[...]
    for step in range(4):
        store_parts(parts, mm_nt(grad_heads, w_in[step][...]), step, rows)
    store_sums(parts, stat, rows)


def feed_weights_kernel(rows, width, count, *refs):
    normed, grad_pair, hidden, grads = (
        refs[:count],
        refs[count : 2 * count],
        refs[2 * count : 3 * count],
        refs[3 * count : 7 * count],
    )
    pair_mine, pair_other, down_mine, down_other = refs[7 * count :]
    units = down_mine.shape[1]
    for half, pair_ref, down_ref in ((1, pair_other, down_other), (0, pair_mine, down_mine)):
        for step in range(4):
            pair_ref[step] = narrow(
                sum(
                    mm_tn(
                        normed[m][:, step * width : (step + 1) * width],
                        grad_pair[m][:, 2 * half * units : 2 * (half + 1) * units],
                    )
                    for m in range(count)
                )
            )
            down_ref[step] = narrow(
                sum(
                    mm_tn(
                        hidden[m][
                            b * rows : (b + 1) * rows, half * units : (half + 1) * units
                        ],
                        grads[4 * m + b][step],
                    )
                    for m in range(count)
                    for b in range(4)
                )
            )


def attend_weights_kernel(rows, width, count, *refs):
    place_ref, refs = (refs[0], refs[1:])
    normed, grad_heads, attn, grads = (
        refs[:count],
        refs[count : 2 * count],
        refs[2 * count : 3 * count],
        refs[3 * count : 19 * count],
    )
    mine_ref, other_ref, in_ref, out_ref = refs[19 * count :]
    half = place_ref[1]
    tall = width // 2
    short = HEAD_SIZE // 2
    for step in range(4):
        in_ref[...] = sum(
            mm_tn(normed[m][:, step * width : (step + 1) * width], grad_heads[m][...])
            for m in range(count)
        )
        out_ref[...] = sum(
            mm_tn(
                attn[m][b * rows : (b + 1) * rows, :],
                piece_of(grads[16 * m : 16 * m + 16], b, step),
            )
            for m in range(count)
            for b in range(4)
        )
        for ref, which in ((other_ref, 1 - half), (mine_ref, half)):
            ref[step, :tall, :] = narrow(
                in_ref[pl.ds(pl.multiple_of(which * tall, tall), tall), :]
            )
            ref[step, tall:, :] = narrow(
                out_ref[pl.ds(pl.multiple_of(which * short, short), short), :]
            )


def feed_join_kernel(*refs):
    place_ref, refs = (refs[0], refs[1:])
    pair, down = ((refs[0:4], refs[4:8]), (refs[8:12], refs[12:16]))
    gate_ref, up_ref, down_ref = refs[16:]
    units = down[0][0].shape[0]
    for step in range(4):
        row = lax.rem(place_ref[0] + step, 4)
        for other in range(2):
            half = lax.rem(place_ref[1] + other, 2)
            window = pl.ds(pl.multiple_of((2 * row + half) * units, units), units)
            gate_ref[:, window] = wide(pair[other][step][:, :units])
            up_ref[:, window] = wide(pair[other][step][:, units:])
            down_ref[window, :] = wide(down[other][step][...])


def attend_join_kernel(*refs):
    place_ref, refs = (refs[0], refs[1:])
    pieces = (refs[0:4], refs[4:8])
    query_ref, key_ref, value_ref, out_ref = refs[8:]
    half_width = HEAD_SIZE // 2
    tall = query_ref.shape[0] // 2

    def put(count, head, turned):
        lane = lax.broadcasted_iota(jnp.int32, (128, count), 0)
        target = lax.broadcasted_iota(jnp.int32, (128, count), 1)
        if turned:
            feature = jnp.where(lane < 64, lane, lane - 64 + half_width)
            used = (lane < half_width) | ((lane >= 64) & (lane < 64 + half_width))
        else:
            feature, used = (lane, lane < HEAD_SIZE)
        return narrow(jnp.where((target == head * HEAD_SIZE + feature) & used, 1.0, 0.0))

    for other in range(2):
        half = lax.rem(place_ref[1] + other, 2)
        window = pl.ds(pl.multiple_of(half * tall, tall), tall)
        query, key, value = (0.0, 0.0, 0.0)
        for step in range(4):
            head = lax.rem(place_ref[0] + step, 4)
            piece = pieces[other][step]
            query = query + mm(piece[:tall, 0:128], put(query_ref.shape[1], head, True))
            pair = lax.div(head, 2)
            key = key + mm(piece[:tall, 128:256], put(key_ref.shape[1], pair, True))
            value = value + mm(piece[:tall, 256:384], put(value_ref.shape[1], pair, False))
            start = pl.multiple_of((2 * head + half) * half_width, half_width)
            out_ref[pl.ds(start, half_width), :] = wide(piece[tall:, :])
        query_ref[window, :] = query
        key_ref[window, :] = key
        value_ref[window, :] = value


def after(value, anchor):
    return lax.optimization_barrier((value, anchor))[0]


def relative_blocks(values, col):
    blocks = values.reshape(2, 2, -1)
    blocks = jnp.where((col % 2) == 1, blocks[:, ::-1], blocks)
    return jnp.where((col // 2) == 1, blocks[::-1], blocks).reshape(-1)


def rope_padded(position):
    half_width = HEAD_SIZE // 2
    frequency = ROPE_BASE ** (-(jnp.arange(half_width, dtype=jnp.float32) * 2.0 / HEAD_SIZE))
    angles = position.astype(jnp.float32)[:, None] * frequency[None, :]
    cosine, sine = (jnp.cos(angles), jnp.sin(angles))
    gap = jnp.zeros((position.shape[0], 64 - half_width), jnp.float32)
    return (
        jnp.concatenate([cosine, gap, cosine, gap], axis=1),
        jnp.concatenate([-sine, gap, sine, gap], axis=1),
    )


def row_slice(matrix, start, size):
    return lax.dynamic_slice_in_dim(matrix, start, size, 0)


def col_slice(matrix, start, size):
    return lax.dynamic_slice_in_dim(matrix, start, size, 1)


def split_local(
    tokens,
    segments,
    attn_gain,
    w_query,
    key_weight,
    value_weight,
    w_out,
    ffn_gain,
    w_gate,
    w_up,
    w_down,
    out_grad,
):
    count, rows, width = tokens.shape
    seq_len = 4 * rows
    row, col, half = (lax.axis_index("row"), lax.axis_index("col"), lax.axis_index("dp"))
    place = jnp.stack([row, half]).astype(jnp.int32)
    units = w_gate.shape[1] // 8

    packed = call(
        head_kernel,
        [shaped((width, 384))] + [shaped((width // 2, 384))] * 3,
        place,
        w_query,
        key_weight,
        value_weight,
    )
    gathered_x = [gather_fine(tokens[0])]
    gains = jnp.stack([attn_gain, ffn_gain])
    gain_steps = jnp.stack([gains] + [shift_rows(gains, s) for s in (1, 2, 3)], axis=1)
    gain_one, gain_two = (wide(gain_steps[0]), wide(gain_steps[1]))
    w_in = [packed[0]]
    w_attn = [row_slice(w_out, row * HEAD_SIZE, HEAD_SIZE)]
    for step in (1, 2, 3):
        got = shift_rows(packed[step], step)
        both = jnp.stack([got, swap_dp(got)])
        w_in.append(jnp.where(half == 0, both, both[::-1]).reshape(width, 384))
        w_attn.append(
            shift_rows(row_slice(w_out, ((row + step) % 4) * HEAD_SIZE, HEAD_SIZE), step)
        )
    for m in range(1, count):
        gathered_x.append(gather_fine(tokens[m]))

    pair_mine, pair_other, down_mine, down_other = ([], [], [], [])
    for step in range(4):
        for other in range(2):
            if step and other:
                continue
            base = (2 * ((row + step) % 4) + (half + other) % 2) * units
            pair = jnp.concatenate(
                [col_slice(w_gate, base, units), col_slice(w_up, base, units)], axis=1
            )
            down = row_slice(w_down, base, units)
            if step:
                pair, down = after((pair, down), gathered_x[-1][3])
                pair, down = (shift_rows(pair, step), shift_rows(down, step))
                pair_mine.append(pair)
                down_mine.append(down)
                pair_other.append(swap_dp(pair))
                down_other.append(swap_dp(down))
            else:
                (pair_other if other else pair_mine).append(pair)
                (down_other if other else down_mine).append(down)
    gathered_g = [
        gather_coarse(after(out_grad[m], gathered_x[-1][3])) for m in range(count)
    ]

    key_place = (
        (col ^ jnp.arange(4, dtype=jnp.int32))[:, None] * rows
        + jnp.arange(rows, dtype=jnp.int32)[None, :]
    ).reshape(-1)
    blocks = [shaped((4, rows, width))] * 4
    tall_blocks = [shaped((4, rows + EXCHANGE_ROWS, width))] * 4
    saved, mids = ([], [])
    for m in range(count):
        position = relative_blocks(positions_of(segments[m, 0]), col)
        tables = rope_padded(position)
        result = call(
            functools.partial(attend_kernel, rows, width),
            blocks
            + [
                shaped((seq_len, MODEL_WIDTH)),
                shaped((seq_len, 384)),
                shaped((seq_len, seq_len)),
                shaped((seq_len, 128)),
                shaped((rows, 1), jnp.float32),
            ],
            *gathered_x[m],
            gain_one,
            *w_in,
            *w_attn,
            *tables,
            (key_place - position)[:, None],
            key_place[:, None],
            key_place[None, :],
        )
        mids.append(wide(tokens[m]) + scatter_fine(result[:4]))
        saved.append(tuple(result[4:]) + tables)

    outputs, fed = ([], [])
    for m in range(count):
        gathered_mid = gather_fine(narrow(mids[m]))
        result = pl_feed(
            rows,
            width,
            blocks,
            tall_blocks,
            units,
            gathered_mid,
            gathered_g[m],
            gain_two,
            pair_mine + pair_other + down_mine + down_other,
        )
        grad_parts = scatter_fine(result[4:8])
        outputs.append(narrow(mids[m] + scatter_coarse(result[:4])))
        grad_normed, stat = (grad_parts[:rows], grad_parts[rows, :rows])
        inverse = result[11]
        grad_mid = (
            wide(out_grad[m])
            + inverse * (grad_normed * wide(ffn_gain))
            - mids[m] * (inverse * inverse * stat[:, None] / MODEL_WIDTH)
        )
        gain_part = jnp.sum(grad_normed * mids[m] * inverse, axis=0)
        fed.append((tuple(result[8:11]), grad_mid, gain_part))

    pair_shape, down_shape = ((4, width, 2 * units), (4, units, width))
    feed_grads = call(
        functools.partial(feed_weights_kernel, rows, width, count),
        [shaped(pair_shape), shaped(pair_shape), shaped(down_shape), shaped(down_shape)],
        *[fed[m][0][0] for m in range(count)],
        *[fed[m][0][2] for m in range(count)],
        *[fed[m][0][1] for m in range(count)],
        *[piece for m in range(count) for piece in gathered_g[m]],
    )
    pair_got, down_got = (swap_dp(feed_grads[1]), swap_dp(feed_grads[3]))
    join = [[], [], [], []]
    for step in range(4):
        pair = narrow(wide(feed_grads[0][step]) + wide(pair_got[step]))
        down = narrow(wide(feed_grads[2][step]) + wide(down_got[step]))
        if step:
            pair, down = (shift_rows(pair, 4 - step), shift_rows(down, 4 - step))
        for target, piece in zip(join, (pair, swap_dp(pair), down, swap_dp(down))):
            target.append(piece)
    grad_gate, grad_up, grad_down = call(
        feed_join_kernel,
        [
            shaped(w_gate.shape, jnp.float32),
            shaped(w_up.shape, jnp.float32),
            shaped(w_down.shape, jnp.float32),
        ],
        place,
        *join[0],
        *join[1],
        *join[2],
        *join[3],
    )

    in_grads, grad_heads, gathered_dz = ([], [], [])
    gain_sums = [0.0, 0.0]
    for m in range(count):
        grad_mid = fed[m][1]
        gathered_dz.append(gather_fine(narrow(grad_mid)))
        normed, heads, probs, attn, inverse, cos_t, sin_t = saved[m]
        result = pl_back(
            rows, width, tall_blocks, gathered_dz[m], w_in, w_attn, cos_t, sin_t, heads, probs
        )
        grad_heads.append(result[4])
        grad_parts = scatter_fine(result[:4])
        grad_normed, stat = (grad_parts[:rows], grad_parts[rows, :rows])
        resid = wide(tokens[m])
        in_grads.append(
            grad_mid
            + inverse * (grad_normed * wide(attn_gain))
            - resid * (inverse * inverse * stat[:, None] / MODEL_WIDTH)
        )
        gain_sums[0] = gain_sums[0] + jnp.sum(grad_normed * resid * inverse, axis=0)
        gain_sums[1] = gain_sums[1] + fed[m][2]

    part_shape = (4, width // 2 + HEAD_SIZE // 2, 384)
    attend_grads = pl.pallas_call(
        functools.partial(attend_weights_kernel, rows, width, count),
        out_shape=[shaped(part_shape), shaped(part_shape)],
        in_specs=[pl.BlockSpec(memory_space=pltpu.SMEM)]
        + [pl.BlockSpec(memory_space=pltpu.VMEM)] * (19 * count),
        out_specs=[pl.BlockSpec(memory_space=pltpu.VMEM)] * 2,
        scratch_shapes=[
            pltpu.VMEM((width, 384), jnp.float32),
            pltpu.VMEM((128, width), jnp.float32),
        ],
        cost_estimate=pl.CostEstimate(flops=1 << 31, bytes_accessed=1 << 23, transcendentals=0),
    )(
        place,
        *[saved[m][0] for m in range(count)],
        *grad_heads,
        *[saved[m][3] for m in range(count)],
        *[piece for m in range(count) for piece in gathered_dz[m]],
    )
    got = swap_dp(attend_grads[1])
    mine, other = ([], [])
    for step in range(4):
        piece = narrow(wide(attend_grads[0][step]) + wide(got[step]))
        if step:
            piece = shift_rows(piece, 4 - step)
        mine.append(piece)
        other.append(swap_dp(piece))
    grad_query, grad_key, grad_value, grad_out = call(
        attend_join_kernel,
        [
            shaped(w_query.shape, jnp.float32),
            shaped(key_weight.shape, jnp.float32),
            shaped(value_weight.shape, jnp.float32),
            shaped(w_out.shape, jnp.float32),
        ],
        place,
        *mine,
        *other,
    )

    gain_total = jnp.stack(gain_sums)
    gain_total = gain_total + swap_cols(gain_total, 1)
    gain_total = gain_total + swap_cols(gain_total, 2)
    gain_total = gain_total + swap_dp(gain_total)
    return (
        jnp.stack(outputs),
        jnp.stack(in_grads),
        gain_total[0],
        grad_query,
        grad_key,
        grad_value,
        grad_out,
        gain_total[1],
        grad_gate,
        grad_up,
        grad_down,
    )


def pl_feed(rows, width, blocks, tall_blocks, units, group, grads, gain, weights):
    seq_len = 4 * rows
    outs = (
        blocks
        + tall_blocks
        + [
            shaped((seq_len, MODEL_WIDTH)),
            shaped((seq_len, 2 * units)),
            shaped((seq_len, 4 * units)),
            shaped((rows, 1), jnp.float32),
        ]
    )
    operands = [*group, *grads, gain, *weights]
    return pl.pallas_call(
        functools.partial(feed_kernel, rows, width),
        out_shape=outs,
        in_specs=[pl.BlockSpec(memory_space=pltpu.VMEM)] * len(operands),
        out_specs=[pl.BlockSpec(memory_space=pltpu.VMEM)] * len(outs),
        scratch_shapes=[pltpu.VMEM((seq_len, units), jnp.float32)],
        cost_estimate=pl.CostEstimate(flops=5 << 29, bytes_accessed=1 << 23, transcendentals=0),
    )(*operands)


def pl_back(rows, width, tall_blocks, group, w_in, w_attn, cos_t, sin_t, heads, probs):
    seq_len = 4 * rows
    outs = tall_blocks + [shaped((seq_len, 384))]
    operands = [*group, *w_in, *w_attn, cos_t, sin_t, heads, probs]
    return pl.pallas_call(
        functools.partial(attend_back_kernel, rows, width),
        out_shape=outs,
        in_specs=[pl.BlockSpec(memory_space=pltpu.VMEM)] * len(operands),
        out_specs=[pl.BlockSpec(memory_space=pltpu.VMEM)] * len(outs),
        scratch_shapes=[
            pltpu.VMEM((seq_len, HEAD_SIZE), jnp.bfloat16),
            pltpu.VMEM((seq_len, seq_len), jnp.bfloat16),
        ],
        cost_estimate=pl.CostEstimate(flops=1 << 30, bytes_accessed=1 << 22, transcendentals=0),
    )(*operands)


def fits_split(mesh):
    sizes = (mesh.shape["dp"], mesh.shape["row"], mesh.shape["col"])
    return sizes == (2, 4, 4) and sizes[1] * sizes[2] == QUERY_HEADS


def solution(mesh):
    in_specs = (
        P(None, ("dp", "col"), "row"),
        P(None, "dp", None),
        P("row"),
        P("row", "col"),
        P("row", "col"),
        P("row", "col"),
        P("col", "row"),
        P("row"),
        P("row", "col"),
        P("row", "col"),
        P("col", "row"),
        P(None, ("dp", "col"), "row"),
    )
    out_specs = (
        P(None, ("dp", "col"), "row"),
        P(None, ("dp", "col"), "row"),
        P("row"),
        P("row", "col"),
        P("row", "col"),
        P("row", "col"),
        P("col", "row"),
        P("row"),
        P("row", "col"),
        P("row", "col"),
        P("col", "row"),
    )
    body = split_local if fits_split(mesh) else local
    return jax.shard_map(body, mesh=mesh, in_specs=in_specs, out_specs=out_specs, check_vma=False)
```

```python
import functools

import jax
import jax.numpy as jnp
from jax import lax
from jax.experimental import pallas as pl
from jax.experimental.pallas import tpu as pltpu
from jax.sharding import PartitionSpec as P

MODEL_WIDTH = 1536
QUERY_HEADS = 16
KV_HEAD_COUNT = 8
HEAD_SIZE = 96


EPSILON = 1e-05
ROPE_BASE = 100000.0


def positions_of(seg_ids):
    token_length = seg_ids.shape[0]
    places = jnp.arange(token_length, dtype=jnp.int32)
    previous = jnp.concatenate([seg_ids[:1] - 1, seg_ids[:-1]])
    starts = jnp.where(seg_ids != previous, places, 0)
    return places - lax.cummax(starts, axis=0)


def rope_tables(position):
    half_width = HEAD_SIZE // 2
    frequency = ROPE_BASE ** (-(jnp.arange(half_width, dtype=jnp.float32) * 2.0 / HEAD_SIZE))
    angles = position.astype(jnp.float32)[:, None] * frequency[None, :]
    return (jnp.cos(angles)[:, None, :], jnp.sin(angles)[:, None, :])


def rotate(values, cosine, sine_table, direction):
    half_width = values.shape[-1] // 2
    first_half = values[..., :half_width]
    second_half = values[..., half_width:]
    return jnp.concatenate(
        [
            first_half * cosine - direction * second_half * sine_table,
            second_half * cosine + direction * first_half * sine_table,
        ],
        axis=-1,
    )


def gather_cols(block):
    return lax.all_gather(block, "col", axis=0, tiled=True)


def gather_rows(block):
    return lax.all_gather(block, "row", axis=0, tiled=True)


def sum_rows(gathered, matrix):

    def partial_term(first_row, count_of_rows):
        return jnp.dot(gathered, matrix, preferred_element_type=jnp.float32)

    return lax.psum_scatter(
        partial_term(
            jnp.int32(0), lax.axis_size("row") * (gathered.shape[0] // lax.axis_size("row"))
        ),
        "row",
        scatter_dimension=0,
        tiled=True,
    )


def sum_cols(gathered, matrix):

    def partial_term(first_row, count_of_rows):
        return jnp.dot(gathered, matrix, preferred_element_type=jnp.float32)

    return lax.psum_scatter(
        partial_term(
            jnp.int32(0), lax.axis_size("col") * (gathered.shape[0] // lax.axis_size("col"))
        ),
        "col",
        scatter_dimension=0,
        tiled=True,
    )


def row_total(values):
    return lax.psum(values, "row")


def gather_keys(key_own, value_own):
    return (
        lax.all_gather(key_own, "row", axis=0, tiled=True),
        lax.all_gather(value_own, "row", axis=0, tiled=True),
    )


def scatter_keys(grad_keys, grad_values):
    return (
        lax.psum_scatter(
            grad_keys.astype(jnp.bfloat16), "row", scatter_dimension=0, tiled=True
        ).astype(jnp.float32),
        lax.psum_scatter(
            grad_values.astype(jnp.bfloat16), "row", scatter_dimension=0, tiled=True
        ).astype(jnp.float32),
    )


def weight_grad(left_op, right_op):
    return lax.dot_general(
        left_op, right_op, (((0,), (0,)), ((), ())), preferred_element_type=jnp.float32
    )


def reduce_weights(parts):
    return (
        lax.psum(parts[0].astype(jnp.bfloat16), "dp").astype(jnp.float32),
        lax.psum(parts[1].astype(jnp.bfloat16), "dp").astype(jnp.float32),
        lax.psum(parts[2].astype(jnp.bfloat16), "dp").astype(jnp.float32),
        lax.psum(parts[3].astype(jnp.bfloat16), "dp").astype(jnp.float32),
    )


def reduce_gains(parts):
    return lax.psum((parts[0], parts[1]), ("dp", "col"))


def finish(weight_parts, gain_parts):
    return (reduce_weights(weight_parts), reduce_gains(gain_parts))


def masked_scores(grouped_query, key_heads, allowed):
    scores = jnp.einsum(
        "qcgd,kcd->cgqk", grouped_query, key_heads, preferred_element_type=jnp.float32
    )
    return jnp.where(allowed[None, None], scores, -1e30)


def project_heads(projected, cos_rows, sin_rows, width_query, width_kv):
    count_of_rows = projected.shape[0]
    local_key_value = width_kv // HEAD_SIZE
    query_lin = projected[:, :width_query].reshape(
        count_of_rows, width_query // HEAD_SIZE, HEAD_SIZE
    )
    key_lin = projected[:, width_query : width_query + width_kv].reshape(
        count_of_rows, local_key_value, HEAD_SIZE
    )
    query_rows = (rotate(query_lin, cos_rows, sin_rows, 1.0) * HEAD_SIZE ** (-0.5)).astype(
        jnp.bfloat16
    )
    grouped_query = query_rows.reshape(
        count_of_rows, local_key_value, QUERY_HEADS // KV_HEAD_COUNT, HEAD_SIZE
    )
    key_own = (
        rotate(key_lin, cos_rows, sin_rows, 1.0)
        .astype(jnp.bfloat16)
        .reshape(count_of_rows, width_kv)
    )
    value_own = projected[:, width_query + width_kv :].astype(jnp.bfloat16)
    return (grouped_query, key_own, value_own)


def attend(grouped_query, key_heads, value_heads, allowed):
    scores = masked_scores(grouped_query, key_heads, allowed)
    top_score = jnp.max(scores, axis=-1, keepdims=True)
    exponent = jnp.exp(scores - top_score)
    sum_exp = jnp.sum(exponent, axis=-1, keepdims=True)
    attn_probs = exponent / sum_exp
    attended = jnp.einsum(
        "cgqk,kcd->qcgd",
        attn_probs.astype(jnp.bfloat16),
        value_heads,
        preferred_element_type=jnp.float32,
    )
    count_of_rows = grouped_query.shape[0]
    return (attended.reshape(count_of_rows, -1).astype(jnp.bfloat16), top_score + jnp.log(sum_exp))


def attend_back(grad_attn, grouped_query, key_heads, value_heads, allowed, log_total):
    seq_len = key_heads.shape[0]
    grad_attended = grad_attn.astype(jnp.bfloat16).reshape(grouped_query.shape)
    probs_again = jnp.exp(masked_scores(grouped_query, key_heads, allowed) - log_total)
    grad_probs = jnp.einsum(
        "qcgd,kcd->cgqk", grad_attended, value_heads, preferred_element_type=jnp.float32
    )
    row_delta = jnp.sum(probs_again * grad_probs, axis=-1, keepdims=True)
    grad_scores = (probs_again * (grad_probs - row_delta)).astype(jnp.bfloat16)
    grad_value_all = jnp.einsum(
        "cgqk,qcgd->kcd",
        probs_again.astype(jnp.bfloat16),
        grad_attended,
        preferred_element_type=jnp.float32,
    )
    grad_query = jnp.einsum(
        "cgqk,kcd->qcgd", grad_scores, key_heads, preferred_element_type=jnp.float32
    )
    grad_key_all = jnp.einsum(
        "cgqk,qcgd->kcd", grad_scores, grouped_query, preferred_element_type=jnp.float32
    )
    return (grad_query, grad_key_all.reshape(seq_len, -1), grad_value_all.reshape(seq_len, -1))


def head_grads(grad_query, grad_key_own, grad_value_own, cos_rows, sin_rows):
    count_of_rows = grad_query.shape[0]
    grad_query_lin = rotate(
        grad_query.reshape(count_of_rows, -1, HEAD_SIZE) * HEAD_SIZE ** (-0.5),
        cos_rows,
        sin_rows,
        -1.0,
    )
    grad_key_lin = rotate(
        grad_key_own.reshape(count_of_rows, -1, HEAD_SIZE), cos_rows, sin_rows, -1.0
    )
    return jnp.concatenate(
        [
            grad_query_lin.reshape(count_of_rows, -1),
            grad_key_lin.reshape(count_of_rows, -1),
            grad_value_own,
        ],
        axis=1,
    ).astype(jnp.bfloat16)


def blocked_step(resid_in, grad_top, seg_all, cos_all, sin_all, weight_set, norm_gains, widths):
    w_qkv, w_out, w_pair, w_down = weight_set
    gain_one, gain_two = norm_gains
    width_query, width_kv, width_ff = widths
    seq_len = resid_in.shape[0] * lax.axis_size("col")
    own_rows = seq_len // lax.axis_size("row")
    own_start = lax.axis_index("row") * own_rows
    cos_own = lax.dynamic_slice_in_dim(cos_all, own_start, own_rows, 0)
    sin_own = lax.dynamic_slice_in_dim(sin_all, own_start, own_rows, 0)
    seg_own = lax.dynamic_slice_in_dim(seg_all, own_start, own_rows, 0)
    query_pos = own_start + jnp.arange(own_rows, dtype=jnp.int32)
    key_pos = jnp.arange(seq_len, dtype=jnp.int32)
    allowed = (seg_own[:, None] == seg_all[None, :]) & (key_pos[None, :] <= query_pos[:, None])
    inverse_one = lax.rsqrt(row_total(jnp.sum(resid_in * resid_in, axis=1)) / MODEL_WIDTH + EPSILON)
    first_normed_input = (resid_in * inverse_one[:, None] * gain_one).astype(jnp.bfloat16)
    gathered_one = gather_cols(first_normed_input)
    projected = sum_rows(gathered_one, w_qkv)
    grouped_query, key_own, value_own = project_heads(
        projected, cos_own, sin_own, width_query, width_kv
    )
    key_all, value_all = gather_keys(key_own, value_own)
    key_heads = key_all.reshape(seq_len, -1, HEAD_SIZE)
    value_heads = value_all.reshape(seq_len, -1, HEAD_SIZE)
    attn_rows, log_total = attend(grouped_query, key_heads, value_heads, allowed)
    gathered_attn = gather_rows(attn_rows)
    resid_mid = resid_in + sum_cols(gathered_attn, w_out)
    inverse_two = lax.rsqrt(
        row_total(jnp.sum(resid_mid * resid_mid, axis=1)) / MODEL_WIDTH + EPSILON
    )
    normed_two = (resid_mid * inverse_two[:, None] * gain_two).astype(jnp.bfloat16)
    gathered_two = gather_cols(normed_two)
    pair_lin = sum_rows(gathered_two, w_pair)
    gate_lin = pair_lin[:, :width_ff]
    up_lin = pair_lin[:, width_ff:]
    gate_sig = jax.nn.sigmoid(gate_lin)
    hidden = (gate_lin * gate_sig * up_lin).astype(jnp.bfloat16)
    gathered_hidden = gather_rows(hidden)
    block_out = resid_mid + sum_cols(gathered_hidden, w_down)
    gathered_grad = gather_cols(grad_top)
    grad_hidden = sum_rows(gathered_grad, w_down.T)
    local_down = weight_grad(gathered_hidden, gathered_grad)
    slope_term = gate_sig * (1.0 + gate_lin * (1.0 - gate_sig))
    grad_pair_rows = jnp.concatenate(
        [grad_hidden * up_lin * slope_term, grad_hidden * gate_lin * gate_sig], axis=1
    ).astype(jnp.bfloat16)
    gathered_pair = gather_rows(grad_pair_rows)
    grad_normed_two = sum_cols(gathered_pair, w_pair.T)
    local_pair = weight_grad(gathered_two, gathered_pair)
    scaled_two = grad_normed_two * gain_two
    stat_two = row_total(jnp.sum(scaled_two * resid_mid, axis=1))
    grad_mid = (
        grad_top.astype(jnp.float32)
        + inverse_two[:, None] * scaled_two
        - resid_mid * (inverse_two**3 * stat_two / MODEL_WIDTH)[:, None]
    )
    local_gain_two = jnp.sum(grad_normed_two * resid_mid * inverse_two[:, None], axis=0)
    gathered_mid = gather_cols(grad_mid.astype(jnp.bfloat16))
    grad_attn = sum_rows(gathered_mid, w_out.T)
    local_out = weight_grad(gathered_attn, gathered_mid)
    grad_query, grad_key_all, grad_value_all = attend_back(
        grad_attn, grouped_query, key_heads, value_heads, allowed, log_total
    )
    grad_key_own, grad_value_own = scatter_keys(grad_key_all, grad_value_all)
    grad_qkv_rows = head_grads(grad_query, grad_key_own, grad_value_own, cos_own, sin_own)
    gathered_qkv = gather_rows(grad_qkv_rows)
    grad_normed_one = sum_cols(gathered_qkv, w_qkv.T)
    local_qkv = weight_grad(gathered_one, gathered_qkv)
    scaled_one = grad_normed_one * gain_one
    stat_one = row_total(jnp.sum(scaled_one * resid_in, axis=1))
    grad_input = (
        grad_mid
        + inverse_one[:, None] * scaled_one
        - resid_in * (inverse_one**3 * stat_one / MODEL_WIDTH)[:, None]
    )
    local_gain_one = jnp.sum(grad_normed_one * resid_in * inverse_one[:, None], axis=0)
    return (
        block_out.astype(jnp.bfloat16),
        grad_input,
        (local_qkv, local_out, local_pair, local_down),
        (local_gain_one, local_gain_two),
    )


def local(
    tokens,
    segments,
    attn_gain,
    w_query,
    key_weight,
    value_weight,
    w_out,
    ffn_gain,
    w_gate,
    w_up,
    w_down,
    out_grad,
):
    micro_count = tokens.shape[0]
    width_query = w_query.shape[1]
    width_kv = key_weight.shape[1]
    width_ff = w_gate.shape[1]
    widths = (width_query, width_kv, width_ff)
    w_qkv = jnp.concatenate([w_query, key_weight, value_weight], axis=1)
    w_pair = jnp.concatenate([w_gate, w_up], axis=1)
    step_tokens, step_grads = (tokens, out_grad)
    weight_set = (w_qkv, w_out, w_pair, w_down)
    norm_gains = (attn_gain.astype(jnp.float32), ffn_gain.astype(jnp.float32))
    weight_totals = None
    gain_totals = None
    outputs = []
    in_grads = []
    for micro_step in range(micro_count):
        seg_all = segments[micro_step, 0]
        cos_all, sin_all = rope_tables(positions_of(seg_all))
        resid_in = step_tokens[micro_step].astype(jnp.float32)
        grad_top = step_grads[micro_step]
        results = blocked_step(
            resid_in, grad_top, seg_all, cos_all, sin_all, weight_set, norm_gains, widths
        )
        block_out, grad_input, local_weights, local_gains = results
        outputs.append(block_out)
        in_grads.append(grad_input)
        if weight_totals is None:
            weight_totals = tuple(local_weights)
            gain_totals = tuple(local_gains)
        else:
            weight_totals = tuple(
                (
                    total_part + local_part
                    for total_part, local_part in zip(weight_totals, local_weights)
                )
            )
            gain_totals = tuple(
                (
                    total_part + local_part
                    for total_part, local_part in zip(gain_totals, local_gains)
                )
            )
    weight_totals, gain_totals = finish(weight_totals, gain_totals)
    out_stack = jnp.stack(outputs)
    grad_stack = jnp.stack(in_grads)
    grad_qkv_total = weight_totals[0]
    grad_pair_total = weight_totals[2]
    return (
        out_stack,
        grad_stack,
        gain_totals[0],
        grad_qkv_total[:, :width_query],
        grad_qkv_total[:, width_query : width_query + width_kv],
        grad_qkv_total[:, width_query + width_kv :],
        weight_totals[1],
        gain_totals[1],
        grad_pair_total[:, :width_ff],
        grad_pair_total[:, width_ff:],
        weight_totals[3],
    )

EXCHANGE_ROWS = 16


def shift_rows(block, step):
    size = lax.axis_size("row")
    return lax.ppermute(block, "row", [(i, (i + step) % size) for i in range(size)])


def swap_cols(block, mask):
    return lax.ppermute(block, "col", [(i, i ^ mask) for i in range(lax.axis_size("col"))])


def swap_dp(block):
    return lax.ppermute(block, "dp", [(0, 1), (1, 0)])


def gather_blocks(block):
    own = jnp.stack([block] + [shift_rows(block, step) for step in (1, 2, 3)])
    across = swap_cols(own, 2)
    return [own, swap_cols(own, 1), across, swap_cols(across, 1)]


def wide(value):
    return value.astype(jnp.float32)


def narrow(value):
    return value.astype(jnp.bfloat16)


def scatter_blocks(parts):
    own_part, pair_part, across_part, far_part = parts
    from_far = swap_cols(far_part, 1)
    from_pair = swap_cols(pair_part, 1)
    sent = swap_cols(narrow(wide(across_part) + wide(from_far)), 2)
    piece = wide(own_part) + wide(from_pair) + wide(sent)
    total = piece[0]
    for step in (1, 2, 3):
        total = total + wide(shift_rows(narrow(piece[step]), step))
    return total


def mm(left, right):
    return lax.dot_general(
        left, right, (((1,), (0,)), ((), ())), preferred_element_type=jnp.float32
    )


def mm_nt(left, right):
    return lax.dot_general(
        left, right, (((1,), (1,)), ((), ())), preferred_element_type=jnp.float32
    )


def mm_tn(left, right):
    return lax.dot_general(
        left, right, (((0,), (0,)), ((), ())), preferred_element_type=jnp.float32
    )


def call(body, outs, *operands, flops=1 << 30, scratch=(), specs=None):
    moved = sum(o.size * o.dtype.itemsize for o in operands)
    moved += sum(o.size * o.dtype.itemsize for o in outs)
    given = specs or {}
    in_specs = [
        given.get(
            i, pl.BlockSpec(memory_space=pltpu.SMEM if o.ndim == 1 else pltpu.VMEM)
        )
        for i, o in enumerate(operands)
    ]
    return pl.pallas_call(
        body,
        out_shape=outs,
        in_specs=in_specs,
        out_specs=[pl.BlockSpec(memory_space=pltpu.VMEM) for _ in outs],
        scratch_shapes=scratch,
        grid=(1,) if given else (),
        cost_estimate=pl.CostEstimate(flops=flops, bytes_accessed=moved, transcendentals=0),
    )(*operands)


def shaped(shape, dtype=jnp.bfloat16):
    return jax.ShapeDtypeStruct(shape, dtype)


def piece_of(group, block, step):
    if len(group[block].shape) == 4:
        return group[block][step, 0]
    return group[block][step]


def normed_blocks(group, gain_ref, which, normed_ref, own_ref, rows, width):
    for block in range(4):
        pieces = [wide(piece_of(group, block, step)) for step in range(4)]
        square = sum(jnp.sum(p * p, axis=1, keepdims=True) for p in pieces)
        inverse = lax.rsqrt(square / MODEL_WIDTH + EPSILON)
        if block == 0:
            own_ref[...] = inverse
        for step in range(4):
            normed_ref[block * rows : (block + 1) * rows, step * width : (step + 1) * width] = (
                narrow(pieces[step] * inverse * gain_ref[which, step : step + 1, :])
            )


def store_parts(refs, product, step, rows):
    for block in range(4):
        refs[block][(4 - step) % 4, :rows, :] = narrow(product[block * rows : (block + 1) * rows])


def store_sums(refs, products, rows):
    ones = jnp.ones((8, products.shape[1]), jnp.bfloat16)
    high = narrow(products)
    low = narrow(products - wide(high))
    sums = mm_nt(ones, high) + mm_nt(ones, low)
    for block in range(4):
        for step in range(4):
            refs[block][step, rows:, :] = jnp.zeros(
                (EXCHANGE_ROWS, refs[block].shape[2]), jnp.bfloat16
            )
            refs[block][step, rows : rows + 1, :rows] = narrow(
                sums[0:1, block * rows : (block + 1) * rows]
            )


def head_pack_kernel(place_ref, wq_ref, wk_ref, wv_ref, wo_ref, gain_ref, own_ref, *sent_refs):
    row = place_ref[0]
    half = place_ref[1]
    half_width = HEAD_SIZE // 2
    tall = wq_ref.shape[0] // 2

    def pick(count, head, turned):
        source = lax.broadcasted_iota(jnp.int32, (count, 128), 0)
        lane = lax.broadcasted_iota(jnp.int32, (count, 128), 1)
        if turned:
            feature = jnp.where(lane < 64, lane, lane - 64 + half_width)
            used = (lane < half_width) | ((lane >= 64) & (lane < 64 + half_width))
        else:
            feature, used = (lane, lane < HEAD_SIZE)
        return narrow(jnp.where((source == head * HEAD_SIZE + feature) & used, 1.0, 0.0))

    for step, out_ref in enumerate((own_ref,) + sent_refs):
        head = lax.rem(row + step, 4)
        rows = tall if step else 2 * tall
        short = half_width if step else HEAD_SIZE
        window = pl.ds(pl.multiple_of(half * rows, rows), rows) if step else pl.ds(0, rows)
        pair = lax.div(head, 2)
        out_ref[:rows, 0:128] = narrow(mm(wq_ref[window, :], pick(wq_ref.shape[1], head, True)))
        out_ref[:rows, 128:256] = narrow(mm(wk_ref[window, :], pick(wk_ref.shape[1], pair, True)))
        out_ref[:rows, 256:384] = narrow(mm(wv_ref[window, :], pick(wv_ref.shape[1], pair, False)))
        start = head * HEAD_SIZE + (half * half_width if step else 0)
        out_ref[rows : rows + short, :] = wo_ref[
            pl.ds(pl.multiple_of(start, half_width), short), :
        ]
        out_ref[rows + short :, :] = gain_ref[...]


def head_join_kernel(place_ref, own_ref, *refs):
    mine, other = (refs[0:3], refs[3])
    in_ref, attn_ref, gain_ref = refs[4:]
    tall = in_ref.shape[1] // 2
    short = HEAD_SIZE // 2
    in_ref[0] = own_ref[: 2 * tall, :]
    attn_ref[0] = own_ref[2 * tall : 2 * tall + HEAD_SIZE, :]
    gain_ref[0, 0:1, :] = wide(own_ref[2 * tall + HEAD_SIZE : 2 * tall + HEAD_SIZE + 1, :])
    gain_ref[1, 0:1, :] = wide(own_ref[2 * tall + HEAD_SIZE + 1 : 2 * tall + HEAD_SIZE + 2, :])
    for step in (1, 2, 3):
        for which in range(2):
            piece = other[step - 1] if which else mine[step - 1][...]
            half = lax.rem(place_ref[1] + which, 2)
            in_ref[step, pl.ds(pl.multiple_of(half * tall, tall), tall), :] = piece[:tall]
            attn_ref[step, pl.ds(pl.multiple_of(half * short, short), short), :] = piece[
                tall : tall + short
            ]
        gains = wide(mine[step - 1][tall + short :, :])
        gain_ref[0, step : step + 1, :] = gains[0:1]
        gain_ref[1, step : step + 1, :] = gains[1:2]


def feed_pack_kernel(place_ref, gate_ref, up_ref, down_ref, own_ref, *sent_refs):
    units = own_ref.shape[2] // 3
    for step in range(4):
        for other in range(1 if step else 2):
            unit = 2 * lax.rem(place_ref[0] + step, 4) + lax.rem(place_ref[1] + other, 2)
            window = pl.ds(pl.multiple_of(unit * units, units), units)
            target = sent_refs[step - 1] if step else own_ref.at[other]
            target[:, :units] = gate_ref[:, window]
            target[:, units : 2 * units] = up_ref[:, window]
            for tile in range(3):
                target[tile * units : (tile + 1) * units, 2 * units :] = down_ref[
                    window, tile * units : (tile + 1) * units
                ]


def attend_kernel(rows, width, *refs):
    group, refs = (refs[:4], refs[4:])
    w_in, w_out, gain_ref, refs = (refs[0], refs[1], refs[2], refs[3:])
    cos_ref, sin_ref, start_ref, place_ref, key_ref = refs[:5]
    parts = refs[5:9]
    normed_ref, heads_ref, probs_ref, attn_ref, inverse_ref = refs[9:]
    normed_blocks(group, gain_ref, 0, normed_ref, inverse_ref, rows, width)
    lin = sum(mm(normed_ref[:, s * width : (s + 1) * width], w_in[s]) for s in range(4))
    cos_t = cos_ref[...]
    sin_t = sin_ref[...]
    query, key = (lin[:, :128], lin[:, 128:256])
    query = query * cos_t + pltpu.roll(query, 64, 1) * sin_t
    key = narrow(key * cos_t + pltpu.roll(key, 64, 1) * sin_t)
    heads_ref[:, 0:128] = narrow(query * HEAD_SIZE ** (-0.5))
    heads_ref[:, 128:256] = key
    value = narrow(lin[:, 256:384])
    heads_ref[:, 256:384] = value
    for block in range(4):
        sl = slice(block * rows, (block + 1) * rows)
        scores = mm_nt(heads_ref[sl, 0:128], key)
        allowed = (key_ref[...] >= start_ref[sl, :]) & (key_ref[...] <= place_ref[sl, :])
        scores = jnp.where(allowed, scores, -1e30)
        exponent = jnp.exp(scores - jnp.max(scores, axis=1, keepdims=True))
        probs = narrow(exponent / jnp.sum(exponent, axis=1, keepdims=True))
        probs_ref[sl, :] = probs
        attn_ref[sl, :] = narrow(mm(probs, value))
    attn = attn_ref[:, :HEAD_SIZE]
    for step in range(4):
        store_parts(parts, mm(attn, w_out[step]), step, rows)


def pair_piece(own_ref, mine, other_ref, half, step):
    if step == 0:
        return own_ref[half]
    return other_ref[step - 1] if half else mine[step - 1][...]


def down_tiles(piece):
    units = piece.shape[1] // 3
    return jnp.concatenate(
        [piece[t * units : (t + 1) * units, 2 * units :] for t in range(3)], axis=1
    )


def feed_kernel(rows, width, *refs):
    group, grads, refs = (refs[:4], refs[4:8], refs[8:])
    gain_ref, own_ref, mine, other_ref, refs = (refs[0], refs[1], refs[2:5], refs[5], refs[6:])
    out_parts, grad_parts = (refs[:4], refs[4:8])
    normed_ref, hidden_ref, grad_pair_ref, inverse_ref, stat_ref = refs[8:]
    normed_blocks(group, gain_ref, 1, normed_ref, inverse_ref, rows, width)
    units = own_ref.shape[2] // 3
    for half in range(2):
        pieces = [pair_piece(own_ref, mine, other_ref, half, s) for s in range(4)]
        lin = sum(
            mm(normed_ref[:, s * width : (s + 1) * width], pieces[s][:, : 2 * units])
            for s in range(4)
        )
        gate, up = (lin[:, :units], lin[:, units:])
        downs = [down_tiles(piece) for piece in pieces]
        grad_hidden = jnp.concatenate(
            [sum(mm_nt(piece_of(grads, b, s), downs[s]) for s in range(4)) for b in range(4)],
            axis=0,
        )
        sig = jax.nn.sigmoid(gate)
        hidden_ref[:, half * units : (half + 1) * units] = narrow(gate * sig * up)
        grad_gate = narrow(grad_hidden * up * (sig * (1.0 + gate * (1.0 - sig))))
        grad_up = narrow(grad_hidden * gate * sig)
        grad_pair_ref[:, 2 * half * units : (2 * half + 1) * units] = grad_gate
        grad_pair_ref[:, (2 * half + 1) * units : (2 * half + 2) * units] = grad_up
        term = wide(grad_gate) * gate + wide(grad_up) * up
        if half:
            stat_ref[...] += term
        else:
            stat_ref[...] = term
    for step in range(4):
        pieces = [pair_piece(own_ref, mine, other_ref, half, step) for half in range(2)]
        product = sum(
            mm_nt(
                grad_pair_ref[:, 2 * half * units : 2 * (half + 1) * units],
                pieces[half][:, : 2 * units],
            )
            for half in range(2)
        )
        store_parts(grad_parts, product, step, rows)
        product = sum(
            mm(hidden_ref[:, half * units : (half + 1) * units], down_tiles(pieces[half]))
            for half in range(2)
        )
        store_parts(out_parts, product, step, rows)
    store_sums(grad_parts, stat_ref[...], rows)


def attend_back_kernel(rows, width, *refs):
    group, refs = (refs[:4], refs[4:])
    w_in, w_out, refs = (refs[0], refs[1], refs[2:])
    cos_ref, sin_ref, heads_ref, probs_ref = refs[:4]
    parts = refs[4:8]
    grad_heads_ref, grad_attn_ref, grad_scores_ref = refs[8:]
    for block in range(4):
        grad_attn_ref[block * rows : (block + 1) * rows, :] = narrow(
            sum(mm_nt(piece_of(group, block, s), w_out[s]) for s in range(4))
        )
    grad_attn = grad_attn_ref[...]
    value = heads_ref[:, 256 : 256 + HEAD_SIZE]
    for block in range(4):
        sl = slice(block * rows, (block + 1) * rows)
        probs = wide(probs_ref[sl, :])
        weighted = mm_nt(grad_attn_ref[sl, :], value)
        delta = jnp.sum(probs * weighted, axis=1, keepdims=True)
        grad_scores_ref[sl, :] = narrow(probs * (weighted - delta))
    grad_scores = grad_scores_ref[...]
    query, key = (heads_ref[:, 0:128], heads_ref[:, 128:256])
    grad_query = mm(grad_scores, key)
    grad_key = mm_tn(grad_scores, query)
    grad_value = mm_tn(probs_ref[...], grad_attn)
    stat = grad_query * wide(query) + grad_key * wide(key)
    pad = jnp.zeros((grad_value.shape[0], 128 - HEAD_SIZE), jnp.float32)
    grad_value = jnp.concatenate([grad_value, pad], axis=1)
    stat = stat + grad_value * wide(heads_ref[:, 256:384])
    cos_t = cos_ref[...]
    sin_t = sin_ref[...]
    scale = HEAD_SIZE ** (-0.5)
    grad_heads_ref[:, 0:128] = narrow(
        (grad_query * cos_t - pltpu.roll(grad_query, 64, 1) * sin_t) * scale
    )
    grad_heads_ref[:, 128:256] = narrow(grad_key * cos_t - pltpu.roll(grad_key, 64, 1) * sin_t)
    grad_heads_ref[:, 256:384] = narrow(grad_value)
    grad_heads = grad_heads_ref[...]
    for step in range(4):
        store_parts(parts, mm_nt(grad_heads, w_in[step]), step, rows)
    store_sums(parts, stat, rows)


def feed_weights_kernel(rows, width, count, *refs):
    normed, grad_pair, hidden, grads = (
        refs[:count],
        refs[count : 2 * count],
        refs[2 * count : 3 * count],
        refs[3 * count : 3 * count + 4],
    )
    mine_ref, other_ref = refs[3 * count + 4 :]
    units = mine_ref.shape[2] // 3
    for half, ref in ((1, other_ref), (0, mine_ref)):
        for step in range(4):
            ref[step, :, : 2 * units] = narrow(
                sum(
                    mm_tn(
                        normed[m][:, step * width : (step + 1) * width],
                        grad_pair[m][:, 2 * half * units : 2 * (half + 1) * units],
                    )
                    for m in range(count)
                )
            )
            down = narrow(
                sum(
                    mm_tn(
                        hidden[m][
                            b * rows : (b + 1) * rows, half * units : (half + 1) * units
                        ],
                        grads[b][step, m],
                    )
                    for m in range(count)
                    for b in range(4)
                )
            )
            for tile in range(3):
                ref[step, tile * units : (tile + 1) * units, 2 * units :] = down[
                    :, tile * units : (tile + 1) * units
                ]


def attend_weights_kernel(rows, width, count, *refs):
    place_ref, refs = (refs[0], refs[1:])
    normed, grad_heads, attn, grads = (
        refs[:count],
        refs[count : 2 * count],
        refs[2 * count : 3 * count],
        refs[3 * count : 7 * count],
    )
    mine_ref, other_ref, in_ref, out_ref = refs[7 * count :]
    half = place_ref[1]
    tall = width // 2
    short = HEAD_SIZE // 2
    for step in range(4):
        in_ref[...] = sum(
            mm_tn(normed[m][:, step * width : (step + 1) * width], grad_heads[m][...])
            for m in range(count)
        )
        out_ref[...] = sum(
            mm_tn(
                attn[m][b * rows : (b + 1) * rows, :],
                grads[4 * m + b][step],
            )
            for m in range(count)
            for b in range(4)
        )
        for ref, which in ((other_ref, 1 - half), (mine_ref, half)):
            ref[step, :tall, :] = narrow(
                in_ref[pl.ds(pl.multiple_of(which * tall, tall), tall), :]
            )
            ref[step, tall:, :] = narrow(
                out_ref[pl.ds(pl.multiple_of(which * short, short), short), :]
            )


def feed_join_kernel(place_ref, mine_ref, other_ref, gate_ref, up_ref, down_ref):
    units = mine_ref.shape[2] // 3
    for step in range(4):
        row = lax.rem(place_ref[0] + step, 4)
        for other, ref in enumerate((mine_ref, other_ref)):
            half = lax.rem(place_ref[1] + other, 2)
            window = pl.ds(pl.multiple_of((2 * row + half) * units, units), units)
            gate_ref[:, window] = wide(ref[step, :, :units])
            up_ref[:, window] = wide(ref[step, :, units : 2 * units])
            down_ref[window, :] = wide(down_tiles(ref[step]))


def attend_join_kernel(*refs):
    place_ref, pieces = (refs[0], refs[1:3])
    query_ref, key_ref, value_ref, out_ref = refs[3:]
    half_width = HEAD_SIZE // 2
    tall = query_ref.shape[0] // 2

    def put(count, head, turned):
        lane = lax.broadcasted_iota(jnp.int32, (128, count), 0)
        target = lax.broadcasted_iota(jnp.int32, (128, count), 1)
        if turned:
            feature = jnp.where(lane < 64, lane, lane - 64 + half_width)
            used = (lane < half_width) | ((lane >= 64) & (lane < 64 + half_width))
        else:
            feature, used = (lane, lane < HEAD_SIZE)
        return narrow(jnp.where((target == head * HEAD_SIZE + feature) & used, 1.0, 0.0))

    for other in range(2):
        half = lax.rem(place_ref[1] + other, 2)
        window = pl.ds(pl.multiple_of(half * tall, tall), tall)
        query, key, value = (0.0, 0.0, 0.0)
        for step in range(4):
            head = lax.rem(place_ref[0] + step, 4)
            piece = pieces[other][step]
            query = query + mm(piece[:tall, 0:128], put(query_ref.shape[1], head, True))
            pair = lax.div(head, 2)
            key = key + mm(piece[:tall, 128:256], put(key_ref.shape[1], pair, True))
            value = value + mm(piece[:tall, 256:384], put(value_ref.shape[1], pair, False))
            start = pl.multiple_of((2 * head + half) * half_width, half_width)
            out_ref[pl.ds(start, half_width), :] = wide(piece[tall:, :])
        query_ref[window, :] = query
        key_ref[window, :] = key
        value_ref[window, :] = value


def after(value, anchor):
    return lax.optimization_barrier((value, anchor))[0]


def settle(grads):
    got = swap_dp(grads[1])
    pieces = [narrow(wide(grads[0][step]) + wide(got[step])) for step in range(4)]
    return jnp.stack([pieces[0]] + [shift_rows(pieces[s], 4 - s) for s in (1, 2, 3)])


def relative_blocks(values, col):
    blocks = values.reshape(2, 2, -1)
    blocks = jnp.where((col % 2) == 1, blocks[:, ::-1], blocks)
    return jnp.where((col // 2) == 1, blocks[::-1], blocks).reshape(-1)


def rope_padded(position):
    half_width = HEAD_SIZE // 2
    frequency = ROPE_BASE ** (-(jnp.arange(half_width, dtype=jnp.float32) * 2.0 / HEAD_SIZE))
    angles = position.astype(jnp.float32)[:, None] * frequency[None, :]
    cosine, sine = (jnp.cos(angles), jnp.sin(angles))
    gap = jnp.zeros((position.shape[0], 64 - half_width), jnp.float32)
    return (
        jnp.concatenate([cosine, gap, cosine, gap], axis=1),
        jnp.concatenate([-sine, gap, sine, gap], axis=1),
    )


def split_local(
    tokens,
    segments,
    attn_gain,
    w_query,
    key_weight,
    value_weight,
    w_out,
    ffn_gain,
    w_gate,
    w_up,
    w_down,
    out_grad,
):
    count, rows, width = tokens.shape
    seq_len = 4 * rows
    row, col, half = (lax.axis_index("row"), lax.axis_index("col"), lax.axis_index("dp"))
    place = jnp.stack([row, half]).astype(jnp.int32)
    units = w_gate.shape[1] // 8

    gathered_x = [gather_blocks(tokens[0])]
    gains = jnp.pad(jnp.stack([attn_gain, ffn_gain]), ((0, EXCHANGE_ROWS - 2), (0, 0)))
    tall = width // 2 + HEAD_SIZE // 2 + EXCHANGE_ROWS
    packed = call(
        head_pack_kernel,
        [shaped((width + HEAD_SIZE + EXCHANGE_ROWS, 384))] + [shaped((tall, 384))] * 3,
        place,
        w_query,
        key_weight,
        value_weight,
        w_out,
        gains,
    )
    moved = [shift_rows(packed[step], step) for step in (1, 2, 3)]
    w_in, w_attn, gain_rows = call(
        head_join_kernel,
        [
            shaped((4, width, 384)),
            shaped((4, HEAD_SIZE, width)),
            shaped((2, 4, width), jnp.float32),
        ],
        place,
        packed[0],
        *moved,
        swap_dp(jnp.stack(moved)),
    )
    for m in range(1, count):
        gathered_x.append(gather_blocks(tokens[m]))
    packed = call(
        feed_pack_kernel,
        [shaped((2, width, 3 * units))] + [shaped((width, 3 * units))] * 3,
        place,
        w_gate,
        w_up,
        w_down,
    )
    moved = [shift_rows(after(packed[s], gathered_x[-1][0]), s) for s in (1, 2, 3)]
    feed_set = [packed[0], *moved, swap_dp(jnp.stack(moved))]
    gathered_g = gather_blocks(after(out_grad, gathered_x[-1][0]))

    key_place = (
        (col ^ jnp.arange(4, dtype=jnp.int32))[:, None] * rows
        + jnp.arange(rows, dtype=jnp.int32)[None, :]
    ).reshape(-1)
    blocks = [shaped((4, rows, width))] * 4
    tall_blocks = [shaped((4, rows + EXCHANGE_ROWS, width))] * 4
    saved, mids = ([], [])
    for m in range(count):
        position = relative_blocks(positions_of(segments[m, 0]), col)
        tables = rope_padded(position)
        result = call(
            functools.partial(attend_kernel, rows, width),
            blocks
            + [
                shaped((seq_len, MODEL_WIDTH)),
                shaped((seq_len, 384)),
                shaped((seq_len, seq_len)),
                shaped((seq_len, 128)),
                shaped((rows, 1), jnp.float32),
            ],
            *gathered_x[m],
            w_in,
            w_attn,
            gain_rows,
            *tables,
            (key_place - position)[:, None],
            key_place[:, None],
            key_place[None, :],
        )
        mids.append(wide(tokens[m]) + scatter_blocks(result[:4]))
        saved.append(tuple(result[4:]) + tables)

    outputs, fed = ([], [])
    for m in range(count):
        gathered_mid = gather_blocks(narrow(mids[m]))
        one_batch = pl.BlockSpec((4, 1, rows, width), lambda i, m=m: (0, m, 0, 0))
        result = call(
            functools.partial(feed_kernel, rows, width),
            blocks
            + tall_blocks
            + [
                shaped((seq_len, MODEL_WIDTH)),
                shaped((seq_len, 2 * units)),
                shaped((seq_len, 4 * units)),
                shaped((rows, 1), jnp.float32),
            ],
            *gathered_mid,
            *gathered_g,
            gain_rows,
            *feed_set,
            flops=5 << 29,
            scratch=[pltpu.VMEM((seq_len, units), jnp.float32)],
            specs={4 + b: one_batch for b in range(4)},
        )
        grad_parts = scatter_blocks(result[4:8])
        outputs.append(narrow(mids[m] + scatter_blocks(result[:4])))
        grad_normed, stat = (grad_parts[:rows], grad_parts[rows, :rows])
        inverse = result[11]
        grad_mid = (
            wide(out_grad[m])
            + inverse * (grad_normed * wide(ffn_gain))
            - mids[m] * (inverse * inverse * stat[:, None] / MODEL_WIDTH)
        )
        gain_part = jnp.sum(grad_normed * mids[m] * inverse, axis=0)
        fed.append((tuple(result[8:11]), grad_mid, gain_part))

    feed_shape = (4, width, 3 * units)
    feed_grads = call(
        functools.partial(feed_weights_kernel, rows, width, count),
        [shaped(feed_shape), shaped(feed_shape)],
        *[fed[m][0][0] for m in range(count)],
        *[fed[m][0][2] for m in range(count)],
        *[fed[m][0][1] for m in range(count)],
        *gathered_g,
        flops=5 << 30,
    )
    feed_mine = settle(feed_grads)
    grad_gate, grad_up, grad_down = call(
        feed_join_kernel,
        [
            shaped(w_gate.shape, jnp.float32),
            shaped(w_up.shape, jnp.float32),
            shaped(w_down.shape, jnp.float32),
        ],
        place,
        feed_mine,
        swap_dp(feed_mine),
    )

    in_grads, grad_heads, gathered_dz = ([], [], [])
    gain_sums = [0.0, 0.0]
    for m in range(count):
        grad_mid = fed[m][1]
        gathered_dz.append(gather_blocks(narrow(grad_mid)))
        normed, heads, probs, attn, inverse, cos_t, sin_t = saved[m]
        result = call(
            functools.partial(attend_back_kernel, rows, width),
            tall_blocks + [shaped((seq_len, 384))],
            *gathered_dz[m],
            w_in,
            w_attn,
            cos_t,
            sin_t,
            heads,
            probs,
            scratch=[
                pltpu.VMEM((seq_len, HEAD_SIZE), jnp.bfloat16),
                pltpu.VMEM((seq_len, seq_len), jnp.bfloat16),
            ],
        )
        grad_heads.append(result[4])
        grad_parts = scatter_blocks(result[:4])
        grad_normed, stat = (grad_parts[:rows], grad_parts[rows, :rows])
        resid = wide(tokens[m])
        in_grads.append(
            grad_mid
            + inverse * (grad_normed * wide(attn_gain))
            - resid * (inverse * inverse * stat[:, None] / MODEL_WIDTH)
        )
        gain_sums[0] = gain_sums[0] + jnp.sum(grad_normed * resid * inverse, axis=0)
        gain_sums[1] = gain_sums[1] + fed[m][2]

    part_shape = (4, width // 2 + HEAD_SIZE // 2, 384)
    attend_grads = call(
        functools.partial(attend_weights_kernel, rows, width, count),
        [shaped(part_shape), shaped(part_shape)],
        place,
        *[saved[m][0] for m in range(count)],
        *grad_heads,
        *[saved[m][3] for m in range(count)],
        *[piece for m in range(count) for piece in gathered_dz[m]],
        flops=1 << 31,
        scratch=[
            pltpu.VMEM((width, 384), jnp.float32),
            pltpu.VMEM((128, width), jnp.float32),
        ],
    )
    attend_mine = settle(attend_grads)
    grad_query, grad_key, grad_value, grad_out = call(
        attend_join_kernel,
        [
            shaped(w_query.shape, jnp.float32),
            shaped(key_weight.shape, jnp.float32),
            shaped(value_weight.shape, jnp.float32),
            shaped(w_out.shape, jnp.float32),
        ],
        place,
        attend_mine,
        swap_dp(attend_mine),
    )

    gain_total = jnp.stack(gain_sums)
    gain_total = gain_total + swap_cols(gain_total, 1)
    gain_total = gain_total + swap_cols(gain_total, 2)
    gain_total = gain_total + swap_dp(gain_total)
    return (
        jnp.stack(outputs),
        jnp.stack(in_grads),
        gain_total[0],
        grad_query,
        grad_key,
        grad_value,
        grad_out,
        gain_total[1],
        grad_gate,
        grad_up,
        grad_down,
    )


def fits_split(mesh):
    sizes = (mesh.shape["dp"], mesh.shape["row"], mesh.shape["col"])
    return sizes == (2, 4, 4) and sizes[1] * sizes[2] == QUERY_HEADS


def solution(mesh):
    in_specs = (
        P(None, ("dp", "col"), "row"),
        P(None, "dp", None),
        P("row"),
        P("row", "col"),
        P("row", "col"),
        P("row", "col"),
        P("col", "row"),
        P("row"),
        P("row", "col"),
        P("row", "col"),
        P("col", "row"),
        P(None, ("dp", "col"), "row"),
    )
    out_specs = (
        P(None, ("dp", "col"), "row"),
        P(None, ("dp", "col"), "row"),
        P("row"),
        P("row", "col"),
        P("row", "col"),
        P("row", "col"),
        P("col", "row"),
        P("row"),
        P("row", "col"),
        P("row", "col"),
        P("col", "row"),
    )
    body = split_local if fits_split(mesh) else local
    return jax.shard_map(body, mesh=mesh, in_specs=in_specs, out_specs=out_specs, check_vma=False)
```
